256 devices in a mesh: feat: 16 (over y, x), dp: 16 (over z, core).
Axes of the slice: x: 4, y: 4, z: 8, core: 2. Of those that a mesh axis runs over, the one named last changes fastest.
Arguments:
- features: bfloat16 [1024, 32768], P('feat', 'dp'), may hold values from -6 to 6
- neighbors: int32 [32768, 10], P('dp'), may hold values from 0 to 2047
- labels: int32 [32768], P('dp'), may hold values from 0 to 171
- loss_weight: float32 [32768], P('dp'), as said below
- w1_self: bfloat16 [1024, 256], P('feat'), may hold values from -0.1875 to 0.1875
- w1_neigh: bfloat16 [1024, 256], P('feat'), may hold values from -0.1875 to 0.1875
- w2_self: bfloat16 [256, 172], replicated, may hold values from -0.375 to 0.375
- w2_neigh: bfloat16 [256, 172], replicated, may hold values from -0.375 to 0.375
Outputs:
- loss: float32 [], replicated
- grad_w1: float32 [2, 1024, 256], P(None, ('feat', 'dp'))
- grad_w2: float32 [2, 256, 172], replicated
The draws below stay inside these ranges and needn't reach their ends.
Inputs may be any that keep to these rules, and one draw needn't show every extreme that they name: `loss_weight`: positive weights.
All inputs are finite; a program needn't handle non-finite values.
Results may differ from the reference program's by a relative error of at most 0.0055.
Values may be sent and summed in bfloat16 or wider, within the bound.
A program may use at most 128 MiB of HBM per device.

```python
import jax
import jax.numpy as jnp
from jax import lax

FIN = 1024
HID = 256
CLS = 172
FAN = 10
SUB = 2048
NODES = 32768


def draw_loss_weight(key, part):
    position = jnp.arange(NODES, dtype=jnp.float32)
    rising = 1.0 + 2.0 * position / (NODES - 1)
    factor = jnp.exp(jax.random.uniform(key, (NODES,), jnp.float32, -0.7, 0.7))
    return (factor * rising).astype(jnp.float32)


def plant(array, own_key, least, largest):
    longest = array.shape.index(max(array.shape))
    spots = []
    for shift in (0, 1):
        where = [jax.random.randint(jax.random.fold_in(own_key, axis), (), 0, length) for axis, length in enumerate(array.shape)]
        where[longest] = (where[longest] + shift) % array.shape[longest]
        spots.append(tuple(where))
    return array.at[spots[0]].set(least).at[spots[1]].set(largest)


def block_scale(own_key, extent, pieces, least, largest):
    gain = 1.0
    for axis_at, parts in pieces:
        steps = jax.random.uniform(jax.random.fold_in(jax.random.fold_in(own_key, 6), axis_at), (parts,), jnp.float32, least / len(pieces), largest / len(pieces))
        gain = gain * jnp.repeat(jnp.exp(steps), extent[axis_at] // parts).reshape((-1,) + (1,) * (len(extent) - 1 - axis_at))
    return gain


def gaussian(stream_key, extent, scale, most, split=(), kind=jnp.bfloat16):
    result = scale * jax.random.normal(stream_key, extent, jnp.float32)
    if split:
        result = result * block_scale(stream_key, extent, split, -0.22, 0.18)
    return jnp.clip(result, -most, most).astype(kind)


def setup_inputs(seed: int = 0) -> dict:
    key_list = jax.random.split(jax.random.key(seed), 9)
    return {
        "features": gaussian(key_list[0], (FIN, NODES), 1.0, 6.0, ((0, 16), (1, 16))),
        "neighbors": plant(jax.random.randint(key_list[1], (NODES, FAN), 0, SUB), jax.random.fold_in(key_list[1], 1), 0, SUB - 1).astype(jnp.int32),
        "labels": plant(jax.random.randint(key_list[2], (NODES,), 0, CLS), jax.random.fold_in(key_list[2], 1), 0, CLS - 1).astype(jnp.int32),
        "loss_weight": draw_loss_weight(jax.random.fold_in(key_list[8], 71), 0),
        "w1_self": gaussian(key_list[4], (FIN, HID), FIN ** -0.5, 0.1875, ((0, 16),)),
        "w1_neigh": gaussian(key_list[5], (FIN, HID), FIN ** -0.5, 0.1875, ((0, 16),)),
        "w2_self": gaussian(key_list[6], (HID, CLS), HID ** -0.5, 0.375),
        "w2_neigh": gaussian(key_list[7], (HID, CLS), HID ** -0.5, 0.375),
    }


def focal_rows(logits, targets):
    logprob = jax.nn.log_softmax(logits, axis=-1)
    picked = jnp.take_along_axis(logprob, targets[:, None], axis=1)[:, 0]
    chance = jnp.exp(picked)
    return -(1.0 - chance) * (1.0 - chance) * picked

def neighbor_mean(lookup_table, indices):
    total = jnp.zeros((indices.shape[0], lookup_table.shape[1]), jnp.float32)
    for which in range(indices.shape[1]):
        total = total + jnp.take(lookup_table, indices[:, which], axis=0).astype(jnp.float32)
    return total / indices.shape[1]

def adjoint_sum(values, indices, total_rows):
    total = jnp.zeros((total_rows, values.shape[1]), jnp.float32)
    for which in range(indices.shape[1]):
        total = total + jax.ops.segment_sum(values, indices[:, which], num_segments=total_rows)
    return total

def contract_first(left_side, right_side):
    return lax.dot_general(left_side, right_side, (((0,), (0,)), ((), ())), preferred_element_type=jnp.float32)

def contract_last(left_side, right_side):
    return lax.dot_general(left_side, right_side, (((1,), (1,)), ((), ())), preferred_element_type=jnp.float32)

def reference(features, neighbors, labels, loss_weight, w1_self, w1_neigh, w2_self, w2_neigh):
    offsets = (jnp.arange(NODES, dtype=jnp.int32) // SUB * SUB).astype(jnp.int32)
    global_ids = (neighbors + offsets[:, None]).astype(jnp.int32)
    fanout = neighbors.shape[1]
    proj_self = contract_first(features, w1_self)
    proj_neigh = contract_first(features, w1_neigh).astype(jnp.bfloat16)
    first_pre = proj_self + neighbor_mean(proj_neigh, global_ids)
    hidden = jax.nn.relu(first_pre).astype(jnp.bfloat16)
    second_agg = neighbor_mean(hidden, global_ids).astype(jnp.bfloat16)
    logits = jnp.dot(hidden, w2_self, preferred_element_type=jnp.float32) + jnp.dot(second_agg, w2_neigh, preferred_element_type=jnp.float32)
    focal_terms, focal_vjp = jax.vjp(lambda values: focal_rows(values, labels), logits)
    grad_logits = focal_vjp(loss_weight)[0].astype(jnp.bfloat16)
    norm_total = jnp.sum(loss_weight)
    loss = jnp.sum(loss_weight * focal_terms) / norm_total
    grad_w2 = jnp.stack([contract_first(hidden, grad_logits), contract_first(second_agg, grad_logits)]) / norm_total
    hidden_own = contract_last(grad_logits, w2_self)
    agg_grad = contract_last(grad_logits, w2_neigh)
    hidden_grad = hidden_own + adjoint_sum(agg_grad, global_ids, NODES) / fanout
    pre_grad = jnp.where(first_pre > 0, hidden_grad, 0.0).astype(jnp.bfloat16)
    proj_grad = (adjoint_sum(pre_grad.astype(jnp.float32), global_ids, NODES) / fanout).astype(jnp.bfloat16)
    grad_w1 = jnp.stack([jnp.dot(features, pre_grad, preferred_element_type=jnp.float32), jnp.dot(features, proj_grad, preferred_element_type=jnp.float32)]) / norm_total
    return (loss, grad_w1, grad_w2)
```

```python
import jax
import jax.numpy as jnp
from jax import lax
from jax.sharding import PartitionSpec as P


def focal_rows(logits, targets):
    logprob = jax.nn.log_softmax(logits, axis=-1)
    hot = targets[:, None] == jnp.arange(logits.shape[1], dtype=jnp.int32)[None, :]
    picked = jnp.sum(jnp.where(hot, logprob, 0.0), axis=1)
    chance = jnp.exp(picked)
    return -(1.0 - chance) * (1.0 - chance) * picked


def contract(left, right, ld, rd):
    return lax.dot_general(
        left, right, (((ld,), (rd,)), ((), ())), preferred_element_type=jnp.float32
    )


def counts_rows(own_neighbors, sub_rows):
    ids = jnp.arange(sub_rows, dtype=jnp.int32)
    hits = own_neighbors[:, :, None] == ids[None, None, :]
    return jnp.sum(hits.astype(jnp.float32), axis=1).astype(jnp.bfloat16)


def counts_cols(neighbors, begin, count):
    ids = begin + jnp.arange(count, dtype=jnp.int32)
    hits = neighbors.T[:, None, :] == ids[None, :, None]
    return jnp.sum(hits.astype(jnp.float32), axis=0).astype(jnp.bfloat16)


def on_device(features, neighbors, labels, loss_weight, w1_self, w1_neigh, w2_self, w2_neigh):
    feat_count = lax.axis_size("feat")
    sub_rows = neighbors.shape[0]
    own_count = sub_rows // feat_count
    row_start = lax.axis_index("feat") * own_count
    own_neighbors = lax.dynamic_slice_in_dim(neighbors, row_start, own_count, 0)
    own_labels = lax.dynamic_slice_in_dim(labels, row_start, own_count, 0)
    own_weight = lax.dynamic_slice_in_dim(loss_weight, row_start, own_count, 0)
    hidden_width = w1_self.shape[1]
    fanout = neighbors.shape[1]
    reads = counts_rows(own_neighbors, sub_rows)
    readers = counts_cols(neighbors, row_start, own_count)
    own_features = lax.all_to_all(features, "feat", split_axis=1, concat_axis=0, tiled=True)
    weights = lax.all_gather(jnp.concatenate([w1_self, w1_neigh], axis=1), "feat", axis=0, tiled=True)
    projected = contract(own_features, weights, 0, 0)
    proj_self = projected[:, :hidden_width]
    proj_neigh = projected[:, hidden_width:].astype(jnp.bfloat16)
    neigh_table = lax.all_gather(proj_neigh, "feat", axis=0, tiled=True)
    first_pre = proj_self + contract(reads, neigh_table, 1, 0) / fanout
    hidden = jax.nn.relu(first_pre).astype(jnp.bfloat16)
    hidden_table = lax.all_gather(hidden, "feat", axis=0, tiled=True)
    second_agg = (contract(reads, hidden_table, 1, 0) / fanout).astype(jnp.bfloat16)
    logits = contract(hidden, w2_self, 1, 0) + contract(second_agg, w2_neigh, 1, 0)
    focal_terms, focal_vjp = jax.vjp(lambda values: focal_rows(values, own_labels), logits)
    grad_logits = focal_vjp(own_weight)[0].astype(jnp.bfloat16)
    weight_part = jnp.sum(own_weight)
    loss_part = jnp.sum(own_weight * focal_terms)
    norm_total, loss_total = lax.psum((weight_part, loss_part), ("feat", "dp"))
    second_local = jnp.stack(
        [contract(hidden, grad_logits, 0, 0), contract(second_agg, grad_logits, 0, 0)]
    )
    hidden_own = contract(grad_logits, w2_self, 1, 1)
    agg_grad = contract(grad_logits, w2_neigh, 1, 1).astype(jnp.bfloat16)
    agg_table = lax.all_gather(agg_grad, "feat", axis=0, tiled=True)
    hidden_grad = hidden_own + contract(readers, agg_table, 1, 0) / fanout
    pre_grad = jnp.where(first_pre > 0, hidden_grad, 0.0).astype(jnp.bfloat16)
    pre_full = lax.all_gather(pre_grad, "feat", axis=0, tiled=True)
    proj_grad = (contract(readers, pre_full, 1, 0) / fanout).astype(jnp.bfloat16)
    proj_full = lax.all_gather(proj_grad, "feat", axis=0, tiled=True)
    first_local = jnp.stack(
        [contract(features, pre_full, 1, 0), contract(features, proj_full, 1, 0)]
    )
    first_sum = lax.psum_scatter(first_local, "dp", scatter_dimension=1, tiled=True)
    second_sum = lax.psum(second_local, ("feat", "dp"))
    return (loss_total / norm_total, first_sum / norm_total, second_sum / norm_total)


def solution(mesh):
    in_specs = (
        P("feat", "dp"),
        P("dp", None),
        P("dp"),
        P("dp"),
        P("feat", None),
        P("feat", None),
        P(),
        P(),
    )
    out_specs = (P(), P(None, ("feat", "dp"), None), P())
    return jax.shard_map(
        on_device, mesh=mesh, in_specs=in_specs, out_specs=out_specs, check_vma=False
    )
```

```python
import functools

import jax
import jax.numpy as jnp
from jax import lax
from jax.experimental import pallas as pl
from jax.experimental.pallas import tpu as pltpu
from jax.sharding import PartitionSpec as P

BF = jnp.bfloat16
F32 = jnp.float32

(W_X, W_FWD, F_X, PS_X, PN_X, H_X, S_X, HO_X, AG_X, PRE_X, PROJ_X, FX_X,
 D_X, X_X, R1_X, L1_X, R2_X, L2_X, R3_X, R4_X) = range(20)


def dot(a, b, ca, cb):
    return lax.dot_general(a, b, (((ca,), (cb,)), ((), ())), preferred_element_type=F32)


def lanes(p):
    return pl.ds(pl.multiple_of(p * 128, 128), 128)


def kernel(fan, f_hbm, nbr_ref, lab_ref, lw_ref, ws_hbm, wn_hbm, w2s_ref, w2n_ref,
           loss_ref, gw1_ref, gw2_ref,
           B, FX, FO, WG, PSS, PNS, PS, PN, FP, HC, SC, HT, SA, GT, HOS, AGS, HO, AG,
           PP, GS, GR, RSS, RX, GWS, GWR, LSS, LSR, T8, TR, L2S, L2R, AW, sems, lsem):
    me, md = lax.axis_index("feat"), lax.axis_index("dp")
    x, y = lax.rem(me, 4), lax.div(me, 4)
    core, z = lax.rem(md, 2), lax.div(md, 2)
    mate = md + 1 - 2 * core
    inv_fan = 1.0 / fan

    def order(p):
        return lax.rem(p, 4) * 4 + lax.div(p, 4)

    q_me = order(me)

    def loop(n, mine, fn):
        def body(s, carry):
            fn(lax.rem(mine + s, n))
            return carry
        lax.fori_loop(1, n, body, 0)

    def rcopy(row, src, dst, out_slot, in_slot, dev):
        return pltpu.make_async_remote_copy(
            src_ref=src, dst_ref=dst, send_sem=sems.at[row, 0, out_slot],
            recv_sem=sems.at[row, 1, in_slot], device_id=dev,
            device_id_type=pl.DeviceIdType.MESH)

    by_feat = lambda p: (p, md)
    by_dp = lambda d: (me, d)
    by_x = lambda xp: (y * 4 + xp, md)
    by_y = lambda yp: (yp * 4 + x, md)
    by_z = lambda zp: (me, zp * 2 + core)

    def send(row, n, mine, src, dst, dev):
        loop(n, mine, lambda p: rcopy(row, src(p), dst, p, mine, dev(p)).start())

    def wait_recv(row, n, mine, blk, dev):
        loop(n, mine, lambda p: rcopy(row, blk(p), blk(p), p, p, dev(p)).wait_recv())

    def wait_send(row, n, mine, src, dev):
        loop(n, mine, lambda p: rcopy(row, src(p), src(p), p, mine, dev(p)).wait_send())

    mine = [
        pltpu.make_async_copy(ws_hbm, WG.at[0, me], lsem.at[0]),
        pltpu.make_async_copy(wn_hbm, WG.at[1, me], lsem.at[1]),
        pltpu.make_async_copy(f_hbm, FX.at[x], lsem.at[2]),
    ]
    for c in mine:
        c.start()
    bar = pltpu.get_barrier_semaphore()
    mesh_id = pl.DeviceIdType.MESH
    loop(16, me, lambda p: pl.semaphore_signal(bar, 1, device_id=(p, md), device_id_type=mesh_id))
    loop(16, md, lambda d: pl.semaphore_signal(bar, 1, device_id=(me, d), device_id_type=mesh_id))
    for c in mine:
        c.wait()
    pl.semaphore_wait(bar, 30)

    send(W_X, 16, me, lambda p: WG.at[core, me], WG.at[core, me], by_feat)
    send(F_X, 16, me, lambda p: FX.at[x, :, lanes(p)], FO.at[me], by_feat)
    FO[me] = FX[x, :, lanes(me)]
    GT[...] = jnp.zeros_like(GT)
    RSS[...] = jnp.zeros_like(RSS)
    LSS[...] = jnp.zeros_like(LSS)

    iota = lax.broadcasted_iota(jnp.int32, (256, 128), 0).astype(F32).astype(BF)

    def build(t, carry):
        lo = lanes(t)

        def group(g, inner):
            acc = jnp.zeros((256, 128), BF)
            for k in range(fan):
                d = (nbr_ref[pl.ds(k, 1), lo] - g * 256).astype(F32).astype(BF)
                acc = acc + jnp.where(iota == d, BF(1), BF(0))
            B[pl.ds(pl.multiple_of(g * 256, 256), 256), lo] = acc
            return inner

        return lax.fori_loop(0, 8, group, carry)

    lax.fori_loop(0, 11, build, 0)

    def forward(p):
        rcopy(W_X, WG.at[core, p], WG.at[core, p], p, p, by_feat(p)).wait_recv()
        rcopy(W_FWD, WG.at[core, p], WG.at[core, p], p, p, (me, mate)).start()

    loop(16, me, forward)
    lax.fori_loop(11, 16, build, 0)
    wait_recv(F_X, 16, me, lambda p: FO.at[p], by_feat)
    loop(16, me, lambda p: rcopy(
        W_FWD, WG.at[1 - core, p], WG.at[1 - core, p], p, p, (me, mate)).wait_recv())

    fo = FO[...].reshape(1024, 128)
    PSS[...] = dot(WG[0].reshape(1024, 256), fo, 0, 0).reshape(16, 16, 128)
    PNS[...] = dot(WG[1].reshape(1024, 256), fo, 0, 0).astype(BF).reshape(16, 16, 128)
    send(PN_X, 16, me, lambda p: PNS.at[order(p)], PN.at[:, lanes(me)], by_feat)
    send(PS_X, 16, me, lambda p: PSS.at[order(p)], PS.at[:, lanes(me)], by_feat)
    send(FX_X, 4, x, lambda xp: FX.at[x], FX.at[x], by_x)
    PN[:, lanes(me)] = PNS[q_me]
    PS[:, lanes(me)] = PSS[q_me]
    wait_recv(PN_X, 16, me, lambda p: PN.at[:, lanes(p)], by_feat)
    wait_recv(PS_X, 16, me, lambda p: PS.at[:, lanes(p)], by_feat)

    def wide(c):
        return pl.ds(pl.multiple_of(c * 256, 256), 256)

    pn = PN[...]

    def layer1(c, carry):
        pre = PS[:, wide(c)] + dot(pn, B[:, wide(c)], 1, 0) * inv_fan
        FP[:, wide(c)] = pre
        HC[:, wide(c)] = jnp.maximum(pre, 0.0).astype(BF)
        return carry

    lax.fori_loop(0, 8, layer1, 0)
    send(H_X, 16, me, lambda p: HC.at[:, lanes(p)], HT.at[q_me], by_feat)
    HT[q_me] = HC[:, lanes(me)]
    hc = HC[...]

    def layer2(c, carry):
        SC[:, wide(c)] = (dot(hc, B[:, wide(c)], 1, 0) * inv_fan).astype(BF)
        return carry

    lax.fori_loop(0, 8, layer2, 0)
    send(S_X, 16, me, lambda p: SC.at[:, lanes(p)], SA.at[q_me], by_feat)
    SA[q_me] = SC[:, lanes(me)]
    wait_recv(H_X, 16, me, lambda p: HT.at[order(p)], by_feat)
    wait_recv(S_X, 16, me, lambda p: SA.at[order(p)], by_feat)

    ht = HT[...].reshape(256, 128)
    sa = SA[...].reshape(256, 128)
    w2s, w2n = w2s_ref[...], w2n_ref[...]
    logits = dot(w2s, ht, 0, 0) + dot(w2n, sa, 0, 0)
    top = jnp.max(logits, axis=0, keepdims=True)
    shifted = logits - top
    logprob = shifted - jnp.log(jnp.sum(jnp.exp(shifted), axis=0, keepdims=True))
    hot = lax.broadcasted_iota(jnp.int32, logits.shape, 0) == lab_ref[pl.ds(me, 1), :]
    picked = jnp.sum(jnp.where(hot, logprob, 0.0), axis=0, keepdims=True)
    weight = lw_ref[pl.ds(me, 1), :]
    chance = jnp.exp(picked)
    rest = 1.0 - chance
    LSS[0:1, :] = -rest * rest * picked * weight
    LSS[1:2, :] = weight
    slope = weight * (2.0 * rest * chance * picked - rest * rest)
    grad = (slope * (jnp.where(hot, 1.0, 0.0) - jnp.exp(logprob))).astype(BF)
    AGS[...] = dot(w2n, grad, 1, 0).astype(BF).reshape(16, 16, 128)
    send(AG_X, 16, me, lambda p: AGS.at[order(p)], AG.at[:, lanes(me)], by_feat)
    HOS[...] = dot(w2s, grad, 1, 0).reshape(16, 16, 128)
    send(HO_X, 16, me, lambda p: HOS.at[order(p)], HO.at[:, lanes(me)], by_feat)
    AG[:, lanes(me)] = AGS[q_me]
    HO[:, lanes(me)] = HOS[q_me]
    send(L1_X, 16, me, lambda p: LSS, LSR.at[me], by_feat)
    LSR[me] = LSS[...]
    GT[0:grad.shape[0], :] = grad
    gt = GT[...]
    GWS[0:8] = dot(ht, gt, 1, 1).astype(BF).reshape(8, 32, 256)
    GWS[8:16] = dot(sa, gt, 1, 1).astype(BF).reshape(8, 32, 256)
    send(R1_X, 16, me, lambda p: GWS.at[p], GWR.at[me], by_feat)
    GWR[me] = GWS[me]
    wait_recv(AG_X, 16, me, lambda p: AG.at[:, lanes(p)], by_feat)
    wait_recv(HO_X, 16, me, lambda p: HO.at[:, lanes(p)], by_feat)

    ag = AG[...]

    def back1(c, carry):
        hidden_grad = HO[:, wide(c)] + dot(ag, B[wide(c), :], 1, 1) * inv_fan
        PP[0, y, :, wide(c)] = jnp.where(FP[:, wide(c)] > 0, hidden_grad, 0.0).astype(BF)
        return carry

    lax.fori_loop(0, 8, back1, 0)
    send(PRE_X, 4, y, lambda yp: PP.at[0, y], PP.at[0, y], by_y)
    pre = PP[0, y]

    def back2(c, carry):
        PP[1, y, :, wide(c)] = (dot(pre, B[wide(c), :], 1, 1) * inv_fan).astype(BF)
        return carry

    lax.fori_loop(0, 8, back2, 0)
    send(PROJ_X, 4, y, lambda yp: PP.at[1, y], PP.at[1, y], by_y)

    wait_recv(R1_X, 16, me, lambda p: GWR.at[p], by_feat)
    wait_recv(L1_X, 16, me, lambda p: LSR.at[p], by_feat)
    rows = GWR[0].astype(F32)
    part = LSR[0]
    for p in range(1, 16):
        rows = rows + GWR[p].astype(F32)
        part = part + LSR[p]
    for t in range(8):
        T8[t] = rows[8 * (t // 2):8 * (t // 2) + 8, 128 * (t % 2):128 * (t % 2) + 128]
    L2S[...] = part
    send(R2_X, 16, md, lambda d: T8.at[lax.div(d, 2)], TR.at[md], by_dp)
    send(L2_X, 16, md, lambda d: L2S, L2R.at[md], by_dp)
    TR[md] = T8[z]
    L2R[md] = part
    wait_recv(R2_X, 16, md, lambda d: TR.at[d], by_dp)
    AW[me, z] = jnp.sum(TR[...], axis=0)
    send(R3_X, 8, z, lambda zp: AW.at[me, z], AW.at[me, z], by_z)

    wait_recv(FX_X, 4, x, lambda xp: FX.at[xp], by_x)
    wait_recv(PRE_X, 4, y, lambda yp: PP.at[0, yp], by_y)
    wait_recv(PROJ_X, 4, y, lambda yp: PP.at[1, yp], by_y)
    full = dot(FX[...].reshape(256, 2048), PP[...].reshape(128, 2048), 1, 1)
    for d in range(16):
        for xs in range(4):
            GS[d, 4 * xs:4 * xs + 4, :] = full[64 * xs + 4 * d:64 * xs + 4 * d + 4, :]
    send(D_X, 16, md, lambda d: GS.at[d], GR.at[md], by_dp)
    GR[md] = GS[md]

    wait_recv(R3_X, 8, z, lambda zp: AW.at[me, zp], by_z)
    send(R4_X, 16, me, lambda p: AW.at[me], AW.at[me], by_feat)
    wait_recv(L2_X, 16, md, lambda d: L2R.at[d], by_dp)
    totals = jnp.sum(jnp.sum(L2R[...], axis=0), axis=1, keepdims=True)
    loss_total, norm_total = totals[0:1, :], totals[1:2, :]
    scale = 1.0 / norm_total

    wait_recv(D_X, 16, md, lambda d: GR.at[d], by_dp)
    summed = jnp.sum(GR[...], axis=0) * scale
    for xs in range(4):
        RSS[xs, 0:4, :] = summed[4 * xs:4 * xs + 4, :]
    send(X_X, 4, x, lambda xp: RSS.at[xp], RX.at[x], by_x)
    RX[x] = RSS[x]
    loss_ref[...] = jnp.broadcast_to(loss_total / norm_total, loss_ref.shape)
    wait_recv(X_X, 4, x, lambda xp: RX.at[xp], by_x)
    left = lax.broadcasted_iota(jnp.int32, (8, 128), 1) < 64
    for pair in range(2):
        a, b = RX[2 * pair], RX[2 * pair + 1]
        at = slice(128 * pair, 128 * pair + 128)
        gw1_ref[0, :, at] = jnp.where(left, a, pltpu.roll(b, 64, 1))[0:4]
        gw1_ref[1, :, at] = jnp.where(left, pltpu.roll(a, 64, 1), b)[0:4]

    wait_recv(R4_X, 16, me, lambda p: AW.at[p], by_feat)
    for p in range(16):
        for g in range(4):
            at = slice(32 * (p % 8) + 8 * g, 32 * (p % 8) + 8 * g + 8)
            gw2_ref[p // 8, at, 0:128] = AW[p, 2 * g] * scale
            gw2_ref[p // 8, at, 128:] = (AW[p, 2 * g + 1] * scale)[:, 0:gw2_ref.shape[2] - 128]

    wait_send(W_X, 16, me, lambda p: WG.at[core, me], by_feat)
    loop(16, me, lambda p: rcopy(
        W_FWD, WG.at[core, p], WG.at[core, p], p, p, (me, mate)).wait_send())
    wait_send(F_X, 16, me, lambda p: FX.at[x, :, lanes(p)], by_feat)
    for row, src in ((PS_X, PSS), (PN_X, PNS), (HO_X, HOS), (AG_X, AGS)):
        wait_send(row, 16, me, lambda p, src=src: src.at[order(p)], by_feat)
    wait_send(H_X, 16, me, lambda p: HC.at[:, lanes(p)], by_feat)
    wait_send(S_X, 16, me, lambda p: SC.at[:, lanes(p)], by_feat)
    wait_send(L1_X, 16, me, lambda p: LSS, by_feat)
    wait_send(R1_X, 16, me, lambda p: GWS.at[p], by_feat)
    wait_send(FX_X, 4, x, lambda xp: FX.at[x], by_x)
    wait_send(PRE_X, 4, y, lambda yp: PP.at[0, y], by_y)
    wait_send(PROJ_X, 4, y, lambda yp: PP.at[1, y], by_y)
    wait_send(R2_X, 16, md, lambda d: T8.at[lax.div(d, 2)], by_dp)
    wait_send(L2_X, 16, md, lambda d: L2S, by_dp)
    wait_send(R3_X, 8, z, lambda zp: AW.at[me, z], by_z)
    wait_send(R4_X, 16, me, lambda p: AW.at[me], by_feat)
    wait_send(D_X, 16, md, lambda d: GS.at[d], by_dp)
    wait_send(X_X, 4, x, lambda xp: RSS.at[xp], by_x)


def on_device(features, neighbors, labels, loss_weight, w1_self, w1_neigh, w2_self, w2_neigh):
    fan = neighbors.shape[1]
    vmem = pl.BlockSpec(memory_space=pltpu.VMEM)
    hbm = pl.BlockSpec(memory_space=pl.ANY)
    S = pltpu.VMEM
    loss, grad_w1, grad_w2 = pl.pallas_call(
        functools.partial(kernel, fan),
        out_shape=(
            jax.ShapeDtypeStruct((8, 128), F32),
            jax.ShapeDtypeStruct((2, 4, 256), F32),
            jax.ShapeDtypeStruct((2, 256, w2_self.shape[1]), F32),
        ),
        in_specs=[hbm, vmem, vmem, vmem, hbm, hbm, vmem, vmem],
        out_specs=(vmem, vmem, vmem),
        scratch_shapes=[
            S((2048, 2048), BF),
            S((4, 64, 2048), BF),
            S((16, 64, 128), BF),
            S((2, 16, 64, 256), BF),
            S((16, 16, 128), F32),
            S((16, 16, 128), BF),
            S((16, 2048), F32),
            S((16, 2048), BF),
            S((16, 2048), F32),
            S((16, 2048), BF),
            S((16, 2048), BF),
            S((16, 16, 128), BF),
            S((16, 16, 128), BF),
            S((256, 128), BF),
            S((16, 16, 128), F32),
            S((16, 16, 128), BF),
            S((16, 2048), F32),
            S((16, 2048), BF),
            S((2, 4, 16, 2048), BF),
            S((16, 16, 128), F32),
            S((16, 16, 128), F32),
            S((4, 8, 128), F32),
            S((4, 8, 128), F32),
            S((16, 32, 256), BF),
            S((16, 32, 256), BF),
            S((8, 128), F32),
            S((16, 8, 128), F32),
            S((8, 8, 128), F32),
            S((16, 8, 128), F32),
            S((8, 128), F32),
            S((16, 8, 128), F32),
            S((16, 8, 8, 128), F32),
            pltpu.SemaphoreType.DMA((20, 2, 16)),
            pltpu.SemaphoreType.DMA((3,)),
        ],
        compiler_params=pltpu.CompilerParams(
            collective_id=0, has_side_effects=True, vmem_limit_bytes=40 * 2 ** 20),
        name="sage_step",
    )(features, neighbors.T, labels.reshape(16, 128), loss_weight.reshape(16, 128),
      w1_self, w1_neigh, w2_self, w2_neigh)
    return loss[0, 0], grad_w1, grad_w2


def solution(mesh):
    in_specs = (
        P("feat", "dp"),
        P("dp", None),
        P("dp"),
        P("dp"),
        P("feat", None),
        P("feat", None),
        P(),
        P(),
    )
    out_specs = (P(), P(None, ("feat", "dp"), None), P())
    return jax.shard_map(
        on_device, mesh=mesh, in_specs=in_specs, out_specs=out_specs, check_vma=False
    )
```

```python
import functools

import jax
import jax.numpy as jnp
from jax import lax
from jax.experimental import pallas as pl
from jax.experimental.pallas import tpu as pltpu
from jax.sharding import PartitionSpec as P

BF = jnp.bfloat16
F32 = jnp.float32

(WA_X, WB_X, WC_X, WD_X, FWD_X, F_X, PS_X, PN_X, H_X, S_X, HO_X, AG_X, PRE_X, PROJ_X, FX_X, FY_X,
 D_X, X_X, R1_X, L1_X, R2_X, L2_X, R3_X, R4_X) = range(24)


def dot(a, b, ca, cb):
    return lax.dot_general(a, b, (((ca,), (cb,)), ((), ())), preferred_element_type=F32)


def lanes(p, width=128):
    return pl.ds(pl.multiple_of(p * width, width), width)


def kernel(fan, f_hbm, nbr_hbm, lab_hbm, lw_hbm, ws_hbm, wn_hbm, w2s_hbm, w2n_hbm,
           loss_ref, gw1_ref, gw2_ref,
           B, FX, FO, WG, PSS, PNS, PS, PN, FP, HC, SC, HT, SA, GT, HOS, AGS, HO, AG,
           PP, GS, GR, RSS, RX, GWS, GWR, LSS, LSR, T8, TR, L2S, L2R, AW,
           nbr_ref, lab_ref, lw_ref, w2s_ref, w2n_ref, sems, lsem):
    me, md = lax.axis_index("feat"), lax.axis_index("dp")
    x, y = lax.rem(me, 4), lax.div(me, 4)
    core, z = lax.rem(md, 2), lax.div(md, 2)
    mate = (me, md + 1 - 2 * core)
    inv_fan = 1.0 / fan

    def order(p):
        return lax.rem(p, 4) * 4 + lax.div(p, 4)

    q_me = order(me)

    near = lambda d, n: min(d, n - d)
    XS = [lax.rem(x + d, 4) for d in (2, 1, 3)]
    YS = [lax.rem(y + d, 4) for d in (2, 1, 3)]
    ZS = [lax.rem(z + d, 8) for d in (4, 3, 5, 2, 6, 1, 7)]
    plane = sorted(((a, b) for a in range(4) for b in range(4) if a or b),
                   key=lambda o: -near(o[0], 4) - near(o[1], 4))
    FEAT = [lax.rem(y + a, 4) * 4 + lax.rem(x + b, 4) for a, b in plane]
    line = sorted(((a, b) for a in range(8) for b in range(2) if a or b),
                  key=lambda o: -near(o[0], 8))
    DP = [lax.rem(z + a, 8) * 2 + (core if b == 0 else 1 - core) for a, b in line]

    def rcopy(row, src, dst, dev):
        return pltpu.make_async_remote_copy(
            src_ref=src, dst_ref=dst, send_sem=sems.at[0, row], recv_sem=sems.at[1, row],
            device_id=dev, device_id_type=pl.DeviceIdType.MESH)

    by_feat = lambda p: (p, md)
    by_dp = lambda d: (me, d)
    by_x = lambda xp: (y * 4 + xp, md)
    by_y = lambda yp: (yp * 4 + x, md)
    by_z = lambda zp: (me, zp * 2 + core)
    drains = []

    def owe(row, view):
        drains.append(lambda: rcopy(row, view, view, mate).wait_send())

    def send(row, peers, src, dst, dev, view):
        for p in peers:
            rcopy(row, src(p), dst, dev(p)).start()
        owe(row, view)

    def wait_recv(row, view):
        rcopy(row, view, view, mate).wait_recv()

    bar = pltpu.get_barrier_semaphore()
    mesh_id = pl.DeviceIdType.MESH
    for p in FEAT:
        pl.semaphore_signal(bar, 1, device_id=by_feat(p), device_id_type=mesh_id)
    for d in DP:
        pl.semaphore_signal(bar, 1, device_id=by_dp(d), device_id_type=mesh_id)

    local = [
        pltpu.make_async_copy(f_hbm, FX.at[x], lsem.at[1]),
        pltpu.make_async_copy(nbr_hbm, nbr_ref, lsem.at[2]),
        pltpu.make_async_copy(lab_hbm, lab_ref, lsem.at[3]),
        pltpu.make_async_copy(lw_hbm, lw_ref, lsem.at[4]),
        pltpu.make_async_copy(w2s_hbm, w2s_ref, lsem.at[5]),
        pltpu.make_async_copy(w2n_hbm, w2n_ref, lsem.at[6]),
    ]
    own_w = pltpu.make_async_copy(ws_hbm, WG.at[core, y, x], lsem.at[0])

    @pl.when(core == 0)
    def _():
        own_w.start()

    @pl.when(core == 1)
    def _():
        pltpu.make_async_copy(wn_hbm, WG.at[core, y, x], lsem.at[0]).start()

    for c in local:
        c.start()
    own_w.wait()
    local[0].wait()
    pl.semaphore_wait(bar, 30)

    upper, lower = WG.at[core, y, x, 0:32], WG.at[core, y, x, 32:64]
    send(WA_X, XS, lambda xp: upper, upper, by_x, WG.at[0, 0, 0:3, 0:32])
    send(WB_X, YS, lambda yp: lower, lower, by_y, WG.at[0, 0, 0:3, 32:64])
    send(F_X, FEAT, lambda p: FX.at[x, :, lanes(p)], FO.at[me], by_feat, FO.at[0:15])
    for c in local[1:]:
        c.wait()
    FO[me] = FX[x, :, lanes(me)]
    GT[...] = jnp.zeros_like(GT)
    RSS[...] = jnp.zeros_like(RSS)
    LSS[...] = jnp.zeros_like(LSS)

    iota = lax.broadcasted_iota(jnp.int32, (256, 128), 0).astype(F32).astype(BF).reshape(16, 16, 128)

    def spread(row):
        return jnp.broadcast_to(row.astype(F32), (16, 128)).astype(BF)

    def build(t, carry):
        lo = lanes(t)
        ids = nbr_ref[:, lo]
        times = jnp.zeros((fan, 128), F32)
        for k in range(fan):
            times = times + jnp.where(ids == ids[k:k + 1], 1.0, 0.0)
        count = [spread(times[k:k + 1]) for k in range(fan)]
        low = [spread(ids[k:k + 1] & 255) for k in range(fan)]
        high = [spread(ids[k:k + 1] >> 8) for k in range(fan)]

        def group(g, inner):
            here = jnp.full((16, 128), g, jnp.int32).astype(F32).astype(BF)
            acc = jnp.zeros((16, 16, 128), BF)
            for k in range(fan):
                at = jnp.where(high[k] == here, low[k], BF(300))
                acc = jnp.where(iota == at[None], count[k][None], acc)
            B[lanes(g, 256), lo] = acc.reshape(256, 128)
            return inner

        return lax.fori_loop(0, 8, group, carry)

    lax.fori_loop(0, 6, build, 0)
    wait_recv(WA_X, WG.at[0, 0, 0:3, 0:32])
    wait_recv(WB_X, WG.at[0, 0, 0:3, 32:64])
    uppers, lowers = WG.at[core, y, :, 0:32], WG.at[core, :, x, 32:64]
    for ready in (uppers, lowers):
        rcopy(FWD_X, ready, ready, mate).start()
    send(WC_X, YS, lambda yp: uppers, uppers, by_y, WG.at[0, 0:3, :, 0:32])
    send(WD_X, XS, lambda xp: lowers, lowers, by_x, WG.at[0, :, 0:3, 32:64])
    lax.fori_loop(6, 14, build, 0)
    wait_recv(WC_X, WG.at[0, 0:3, :, 0:32])
    for yp in YS:
        ready = WG.at[core, yp, :, 0:32]
        rcopy(FWD_X, ready, ready, mate).start()
    wait_recv(WD_X, WG.at[0, :, 0:3, 32:64])
    for xp in XS:
        ready = WG.at[core, :, xp, 32:64]
        rcopy(FWD_X, ready, ready, mate).start()
    owe(FWD_X, WG.at[0])
    lax.fori_loop(14, 16, build, 0)
    wait_recv(F_X, FO.at[0:15])
    wait_recv(FWD_X, WG.at[0])

    fo = FO[...].reshape(1024, 128)
    PNS[...] = dot(WG[1].reshape(1024, 256), fo, 0, 0).astype(BF).reshape(16, 16, 128)
    send(PN_X, FEAT, lambda p: PNS.at[order(p)], PN.at[:, lanes(me)], by_feat, PNS.at[0:15])
    PSS[...] = dot(WG[0].reshape(1024, 256), fo, 0, 0).reshape(16, 16, 128)
    send(PS_X, FEAT, lambda p: PSS.at[order(p)], PS.at[:, lanes(me)], by_feat, PSS.at[0:15])
    PN[:, lanes(me)] = PNS[q_me]
    PS[:, lanes(me)] = PSS[q_me]

    def features_to(xp, piece):
        part = FX.at[x, :, lanes(piece, 512)]
        rcopy(FX_X, part, part, by_x(xp)).start()

    ahead, behind = lax.rem(x + 1, 4), lax.rem(x + 3, 4)
    features_to(ahead, 0)
    features_to(behind, 0)
    wait_recv(PN_X, PNS.at[0:15])
    features_to(ahead, 1)
    features_to(behind, 1)
    mean = dot(PN[...], B[...], 1, 0) * inv_fan
    wait_recv(PS_X, PSS.at[0:15])
    first = PS[...] + mean
    FP[...] = first
    hc = jnp.maximum(first, 0.0).astype(BF)
    HC[...] = hc
    send(H_X, FEAT, lambda p: HC.at[:, lanes(p)], HT.at[q_me], by_feat, HT.at[0:15])
    HT[q_me] = HC[:, lanes(me)]

    for s in range(4):
        c = lax.rem(y + 1 + s, 4)
        SC[:, lanes(c, 512)] = (dot(hc, B[:, lanes(c, 512)], 1, 0) * inv_fan).astype(BF)
        for p in (4 * c, 4 * c + 1, 4 * c + 2, 4 * c + 3):
            @pl.when(p != me)
            def _(p=p):
                rcopy(S_X, SC.at[:, lanes(p)], SA.at[q_me], by_feat(p)).start()

    owe(S_X, SA.at[0:15])
    features_to(ahead, 2)
    features_to(behind, 2)
    SA[q_me] = SC[:, lanes(me)]
    wait_recv(H_X, HT.at[0:15])
    ht = HT[...].reshape(256, 128)
    w2s, w2n = w2s_ref[...], w2n_ref[...]
    from_self = dot(w2s, ht, 1, 0)
    wait_recv(S_X, SA.at[0:15])

    sa = SA[...].reshape(256, 128)
    logits = from_self + dot(w2n, sa, 1, 0)
    top = jnp.max(logits, axis=0, keepdims=True)
    shifted = logits - top
    logprob = shifted - jnp.log(jnp.sum(jnp.exp(shifted), axis=0, keepdims=True))
    hot = lax.broadcasted_iota(jnp.int32, logits.shape, 0) == lab_ref[pl.ds(me, 1), :]
    picked = jnp.sum(jnp.where(hot, logprob, 0.0), axis=0, keepdims=True)
    weight = lw_ref[pl.ds(me, 1), :]
    chance = jnp.exp(picked)
    rest = 1.0 - chance
    slope = weight * (2.0 * rest * chance * picked - rest * rest)
    grad = (slope * (jnp.where(hot, 1.0, 0.0) - jnp.exp(logprob))).astype(BF)
    AGS[...] = dot(w2n, grad, 0, 0).astype(BF).reshape(16, 16, 128)
    send(AG_X, FEAT, lambda p: AGS.at[order(p)], AG.at[:, lanes(me)], by_feat, AGS.at[0:15])
    HOS[...] = dot(w2s, grad, 0, 0).reshape(16, 16, 128)
    send(HO_X, FEAT, lambda p: HOS.at[order(p)], HO.at[:, lanes(me)], by_feat, HOS.at[0:15])
    AG[:, lanes(me)] = AGS[q_me]
    HO[:, lanes(me)] = HOS[q_me]
    GT[0:grad.shape[0], :] = grad
    gt = GT[...]
    for part, table in enumerate((ht, sa)):
        second = dot(gt, table, 1, 1).astype(BF)
        for r in range(4):
            for c in range(2):
                GWS[4 * r + 2 * part + c] = second[64 * r:64 * r + 64, 128 * c:128 * c + 128]
    send(R1_X, FEAT, lambda p: GWS.at[p], GWR.at[me], by_feat, GWS.at[0:15])
    GWR[me] = GWS[me]
    LSS[0:1, :] = -rest * rest * picked * weight
    LSS[1:2, :] = weight
    send(L1_X, FEAT, lambda p: LSS, LSR.at[me], by_feat, LSR.at[0:15])
    LSR[me] = LSS[...]
    features_to(ahead, 3)
    features_to(behind, 3)
    owe(FX_X, FX.at[0:2])
    wait_recv(AG_X, AGS.at[0:15])
    wait_recv(FX_X, FX.at[0:2])
    from_behind, from_ahead = FX.at[behind, :, 0:1024], FX.at[ahead, :, 1024:2048]
    rcopy(FY_X, from_behind, from_behind, by_x(ahead)).start()
    rcopy(FY_X, from_ahead, from_ahead, by_x(behind)).start()
    owe(FY_X, FX.at[0])
    from_neigh = dot(AG[...], B[...], 1, 1) * inv_fan
    wait_recv(HO_X, HOS.at[0:15])
    pre = jnp.where(FP[...] > 0, HO[...] + from_neigh, 0.0).astype(BF)
    PP[0, y] = pre
    send(PRE_X, YS, lambda yp: PP.at[0, y], PP.at[0, y], by_y, PP.at[0, 0:3])

    wait_recv(R1_X, GWS.at[0:15])
    wait_recv(L1_X, LSR.at[0:15])
    rows = GWR[0].astype(F32)
    part = LSR[0]
    for p in range(1, 16):
        rows = rows + GWR[p].astype(F32)
        part = part + LSR[p]
    for t in range(8):
        T8[t] = rows[8 * t:8 * t + 8]
    L2S[...] = part
    send(R2_X, DP, lambda d: T8.at[lax.div(d, 2)], TR.at[md], by_dp, TR.at[0:15])
    send(L2_X, DP, lambda d: L2S, L2R.at[md], by_dp, L2R.at[0:15])
    TR[md] = T8[z]
    L2R[md] = part

    for c in range(4):
        at = pl.ds(512 * c, 512)
        PP[1, y, :, at] = (dot(pre, B[at, :], 1, 1) * inv_fan).astype(BF)
        piece = PP.at[1, y, :, at]
        for yp in YS:
            rcopy(PROJ_X, piece, piece, by_y(yp)).start()

    owe(PROJ_X, PP.at[1, 0:3])
    wait_recv(R2_X, TR.at[0:15])
    AW[me, z] = jnp.sum(TR[...], axis=0).astype(BF)
    send(R3_X, ZS, lambda zp: AW.at[me, z], AW.at[me, z], by_z, AW.at[0, 0:7])

    wait_recv(FY_X, FX.at[0])
    wait_recv(PRE_X, PP.at[0, 0:3])
    wait_recv(PROJ_X, PP.at[1, 0:3])
    full = dot(FX[...].reshape(256, 2048), PP[...].reshape(128, 2048), 1, 1)
    for d in range(16):
        for xs in range(4):
            GS[d, 4 * xs:4 * xs + 4, :] = full[64 * xs + 4 * d:64 * xs + 4 * d + 4, :].astype(BF)
    send(D_X, DP, lambda d: GS.at[d], GR.at[md], by_dp, GS.at[0:15])
    GR[md] = GS[md]

    wait_recv(R3_X, AW.at[0, 0:7])
    send(R4_X, FEAT, lambda p: AW.at[me], AW.at[me], by_feat, AW.at[0:15])
    wait_recv(L2_X, L2R.at[0:15])
    totals = jnp.sum(jnp.sum(L2R[...], axis=0), axis=1, keepdims=True)
    loss_total, norm_total = totals[0:1, :], totals[1:2, :]
    scale = 1.0 / norm_total
    loss_ref[...] = loss_total / norm_total

    wait_recv(D_X, GS.at[0:15])
    summed = GR[0].astype(F32)
    for d in range(1, 16):
        summed = summed + GR[d].astype(F32)
    summed = summed * scale
    for xs in range(4):
        RSS[xs, 0:4, :] = summed[4 * xs:4 * xs + 4, :]
    send(X_X, XS, lambda xp: RSS.at[xp], RX.at[x], by_x, RSS.at[0:3])
    RX[x] = RSS[x]
    wait_recv(R4_X, AW.at[0:15])
    classes = gw2_ref.shape[0]
    for p in range(16):
        for t in range(8):
            row = 64 * (p // 4) + 8 * t
            n = min(8, classes - row)
            if n > 0:
                gw2_ref[row:row + n, (p % 4) // 2, 128 * (p % 2):128 * (p % 2) + 128] = (
                    AW[p, t].astype(F32) * scale)[0:n]
    wait_recv(X_X, RSS.at[0:3])
    left = lax.broadcasted_iota(jnp.int32, (8, 128), 1) < 64
    for pair in range(2):
        a, b = RX[2 * pair], RX[2 * pair + 1]
        at = slice(128 * pair, 128 * pair + 128)
        gw1_ref[0, :, at] = jnp.where(left, a, pltpu.roll(b, 64, 1))[0:4]
        gw1_ref[1, :, at] = jnp.where(left, pltpu.roll(a, 64, 1), b)[0:4]
    for wait in drains:
        wait()


def on_device(features, neighbors, labels, loss_weight, w1_self, w1_neigh, w2_self, w2_neigh):
    fan = neighbors.shape[1]
    vmem = pl.BlockSpec(memory_space=pltpu.VMEM)
    hbm = pl.BlockSpec(memory_space=pltpu.HBM)
    S = pltpu.VMEM
    loss, grad_w1, grad_w2 = pl.pallas_call(
        functools.partial(kernel, fan),
        out_shape=(
            jax.ShapeDtypeStruct((1, 1), F32),
            jax.ShapeDtypeStruct((2, 4, 256), F32),
            jax.ShapeDtypeStruct((w2_self.shape[1], 2, 256), F32),
        ),
        in_specs=[hbm] * 8,
        out_specs=(vmem, vmem, vmem),
        scratch_shapes=[
            S((2048, 2048), BF),
            S((4, 64, 2048), BF),
            S((16, 64, 128), BF),
            S((2, 4, 4, 64, 256), BF),
            S((16, 16, 128), F32),
            S((16, 16, 128), BF),
            S((16, 2048), F32),
            S((16, 2048), BF),
            S((16, 2048), F32),
            S((16, 2048), BF),
            S((16, 2048), BF),
            S((16, 16, 128), BF),
            S((16, 16, 128), BF),
            S((256, 128), BF),
            S((16, 16, 128), F32),
            S((16, 16, 128), BF),
            S((16, 2048), F32),
            S((16, 2048), BF),
            S((2, 4, 16, 2048), BF),
            S((16, 16, 128), BF),
            S((16, 16, 128), BF),
            S((4, 8, 128), F32),
            S((4, 8, 128), F32),
            S((16, 64, 128), BF),
            S((16, 64, 128), BF),
            S((8, 128), F32),
            S((16, 8, 128), F32),
            S((8, 8, 128), F32),
            S((16, 8, 128), F32),
            S((8, 128), F32),
            S((16, 8, 128), F32),
            S((16, 8, 8, 128), BF),
            S((fan, 2048), jnp.int32),
            S((16, 128), jnp.int32),
            S((16, 128), F32),
            S(w2_self.shape[::-1], BF),
            S(w2_neigh.shape[::-1], BF),
            pltpu.SemaphoreType.DMA((2, 24)),
            pltpu.SemaphoreType.DMA((7,)),
        ],
        compiler_params=pltpu.CompilerParams(
            collective_id=0, has_side_effects=True, vmem_limit_bytes=40 * 2 ** 20),
        name="sage_step",
    )(*(pltpu.with_memory_space_constraint(a, pltpu.HBM) for a in (
        features, neighbors.T, labels.reshape(16, 128), loss_weight.reshape(16, 128),
        w1_self, w1_neigh, w2_self.T, w2_neigh.T)))
    return loss.reshape(()), grad_w1, grad_w2.transpose(1, 2, 0)


def solution(mesh):
    in_specs = (
        P("feat", "dp"),
        P("dp", None),
        P("dp"),
        P("dp"),
        P("feat", None),
        P("feat", None),
        P(),
        P(),
    )
    out_specs = (P(), P(None, ("feat", "dp"), None), P())
    return jax.shard_map(
        on_device, mesh=mesh, in_specs=in_specs, out_specs=out_specs, check_vma=False
    )
```

```python
import functools

import jax
import jax.numpy as jnp
from jax import lax
from jax.experimental import pallas as pl
from jax.experimental.pallas import tpu as pltpu
from jax.sharding import PartitionSpec as P

BF = jnp.bfloat16
F32 = jnp.float32

(WA_X, WB_X, WC_X, WD_X, FWD_X, F_X, PS_X, PN_X, H_X, S_X, HO_X, AG_X, PRE_X, FX_X, FY_X,
 D_X, X_X, R1_X, L1_X, R2_X, L2_X, R3_X, R4_X) = range(23)


def dot(a, b, ca, cb):
    return lax.dot_general(a, b, (((ca,), (cb,)), ((), ())), preferred_element_type=F32)


def lanes(p, width=128):
    return pl.ds(pl.multiple_of(p * width, width), width)


def kernel(fan, f_hbm, nbr_hbm, lab_hbm, lw_hbm, ws_hbm, wn_hbm, w2s_hbm, w2n_hbm,
           loss_ref, gw1_ref, gw2_ref,
           B, FX, FO, WG, PSS, PNS, PS, PN, FP, HC, SC, HT, SA, GT, HOS, AGS, HO, AG,
           PP, GS, GR, RSS, RX, GWS, GWR, LSS, LSR, T8, TR, L2S, L2R, AW,
           nbr_ref, lab_ref, lw_ref, w2s_ref, w2n_ref, sems, lsem):
    me, md = lax.axis_index("feat"), lax.axis_index("dp")
    x, y = lax.rem(me, 4), lax.div(me, 4)
    core, z = lax.rem(md, 2), lax.div(md, 2)
    mate = (me, md + 1 - 2 * core)
    inv_fan = 1.0 / fan

    def order(p):
        return lax.rem(p, 4) * 4 + lax.div(p, 4)

    q_me = order(me)

    near = lambda d, n: min(d, n - d)
    XS = [lax.rem(x + d, 4) for d in (2, 1, 3)]
    YS = [lax.rem(y + d, 4) for d in (2, 1, 3)]
    ZS = [lax.rem(z + d, 8) for d in (4, 3, 5, 2, 6, 1, 7)]
    plane = sorted(((a, b) for a in range(4) for b in range(4) if a or b),
                   key=lambda o: -near(o[0], 4) - near(o[1], 4))
    FEAT = [lax.rem(y + a, 4) * 4 + lax.rem(x + b, 4) for a, b in plane]
    line = sorted(((a, b) for a in range(8) for b in range(2) if a or b),
                  key=lambda o: -near(o[0], 8))
    DP = [lax.rem(z + a, 8) * 2 + (core if b == 0 else 1 - core) for a, b in line]

    def rcopy(row, src, dst, dev):
        return pltpu.make_async_remote_copy(
            src_ref=src, dst_ref=dst, send_sem=sems.at[0, row], recv_sem=sems.at[1, row],
            device_id=dev, device_id_type=pl.DeviceIdType.MESH)

    by_feat = lambda p: (p, md)
    by_dp = lambda d: (me, d)
    by_x = lambda xp: (y * 4 + xp, md)
    by_y = lambda yp: (yp * 4 + x, md)
    by_z = lambda zp: (me, zp * 2 + core)
    drains = []

    def owe(row, view):
        drains.append(lambda: rcopy(row, view, view, mate).wait_send())

    def send(row, peers, src, dst, dev, view):
        for p in peers:
            rcopy(row, src(p), dst, dev(p)).start()
        owe(row, view)

    def wait_recv(row, view):
        rcopy(row, view, view, mate).wait_recv()

    bar = pltpu.get_barrier_semaphore()
    mesh_id = pl.DeviceIdType.MESH
    for p in FEAT:
        pl.semaphore_signal(bar, 1, device_id=by_feat(p), device_id_type=mesh_id)
    for d in DP:
        pl.semaphore_signal(bar, 1, device_id=by_dp(d), device_id_type=mesh_id)

    local = [
        pltpu.make_async_copy(f_hbm, FX.at[x], lsem.at[1]),
        pltpu.make_async_copy(nbr_hbm, nbr_ref, lsem.at[2]),
        pltpu.make_async_copy(lab_hbm, lab_ref, lsem.at[3]),
        pltpu.make_async_copy(lw_hbm, lw_ref, lsem.at[4]),
        pltpu.make_async_copy(w2s_hbm, w2s_ref, lsem.at[5]),
        pltpu.make_async_copy(w2n_hbm, w2n_ref, lsem.at[6]),
    ]
    own_w = pltpu.make_async_copy(ws_hbm, WG.at[core, y, x], lsem.at[0])

    @pl.when(core == 0)
    def _():
        own_w.start()

    @pl.when(core == 1)
    def _():
        pltpu.make_async_copy(wn_hbm, WG.at[core, y, x], lsem.at[0]).start()

    for c in local:
        c.start()
    own_w.wait()
    local[0].wait()
    pl.semaphore_wait(bar, 30)

    upper, lower = WG.at[core, y, x, 0:32], WG.at[core, y, x, 32:64]
    send(WA_X, XS, lambda xp: upper, upper, by_x, WG.at[0, 0, 0:3, 0:32])
    send(WB_X, YS, lambda yp: lower, lower, by_y, WG.at[0, 0, 0:3, 32:64])
    send(F_X, FEAT, lambda p: FX.at[x, :, lanes(p)], FO.at[me], by_feat, FO.at[0:15])
    for c in local[1:]:
        c.wait()
    FO[me] = FX[x, :, lanes(me)]
    GT[...] = jnp.zeros_like(GT)
    RSS[...] = jnp.zeros_like(RSS)
    LSS[...] = jnp.zeros_like(LSS)

    iota = lax.broadcasted_iota(jnp.int32, (256, 128), 0).astype(F32).astype(BF).reshape(16, 16, 128)

    def spread(row):
        return jnp.broadcast_to(row.astype(F32), (16, 128)).astype(BF)

    def build(t, carry):
        lo = lanes(t)
        ids = nbr_ref[:, lo]
        times = jnp.zeros((fan, 128), F32)
        for k in range(fan):
            times = times + jnp.where(ids == ids[k:k + 1], 1.0, 0.0)
        count = [spread(times[k:k + 1]) for k in range(fan)]
        low = [spread(ids[k:k + 1] & 255) for k in range(fan)]
        high = [spread(ids[k:k + 1] >> 8) for k in range(fan)]

        def group(g, inner):
            here = jnp.full((16, 128), g, jnp.int32).astype(F32).astype(BF)
            acc = jnp.zeros((16, 16, 128), BF)
            for k in range(fan):
                at = jnp.where(high[k] == here, low[k], BF(300))
                acc = jnp.where(iota == at[None], count[k][None], acc)
            B[lanes(g, 256), lo] = acc.reshape(256, 128)
            return inner

        return lax.fori_loop(0, 8, group, carry)

    lax.fori_loop(0, 6, build, 0)
    wait_recv(WA_X, WG.at[0, 0, 0:3, 0:32])
    wait_recv(WB_X, WG.at[0, 0, 0:3, 32:64])
    uppers, lowers = WG.at[core, y, :, 0:32], WG.at[core, :, x, 32:64]
    for ready in (uppers, lowers):
        rcopy(FWD_X, ready, ready, mate).start()
    send(WC_X, YS, lambda yp: uppers, uppers, by_y, WG.at[0, 0:3, :, 0:32])
    send(WD_X, XS, lambda xp: lowers, lowers, by_x, WG.at[0, :, 0:3, 32:64])
    lax.fori_loop(6, 14, build, 0)
    wait_recv(WC_X, WG.at[0, 0:3, :, 0:32])
    for yp in YS:
        ready = WG.at[core, yp, :, 0:32]
        rcopy(FWD_X, ready, ready, mate).start()
    wait_recv(WD_X, WG.at[0, :, 0:3, 32:64])
    for xp in XS:
        ready = WG.at[core, :, xp, 32:64]
        rcopy(FWD_X, ready, ready, mate).start()
    owe(FWD_X, WG.at[0])
    lax.fori_loop(14, 16, build, 0)
    wait_recv(F_X, FO.at[0:15])
    wait_recv(FWD_X, WG.at[0])

    fo = FO[...].reshape(1024, 128)
    PNS[...] = dot(WG[1].reshape(1024, 256), fo, 0, 0).astype(BF).reshape(16, 16, 128)
    send(PN_X, FEAT, lambda p: PNS.at[order(p)], PN.at[:, lanes(me)], by_feat, PNS.at[0:15])
    PSS[...] = dot(WG[0].reshape(1024, 256), fo, 0, 0).reshape(16, 16, 128)
    send(PS_X, FEAT, lambda p: PSS.at[order(p)], PS.at[:, lanes(me)], by_feat, PSS.at[0:15])
    PN[:, lanes(me)] = PNS[q_me]
    PS[:, lanes(me)] = PSS[q_me]

    def features_to(xp, piece):
        part = FX.at[x, :, lanes(piece, 512)]
        rcopy(FX_X, part, part, by_x(xp)).start()

    ahead, behind = lax.rem(x + 1, 4), lax.rem(x + 3, 4)
    features_to(ahead, 0)
    features_to(behind, 0)
    wait_recv(PN_X, PNS.at[0:15])
    features_to(ahead, 1)
    features_to(behind, 1)
    mean = dot(PN[...], B[...], 1, 0) * inv_fan
    wait_recv(PS_X, PSS.at[0:15])
    first = PS[...] + mean
    FP[...] = first
    hc = jnp.maximum(first, 0.0).astype(BF)
    HC[...] = hc
    send(H_X, FEAT, lambda p: HC.at[:, lanes(p)], HT.at[q_me], by_feat, HT.at[0:15])
    HT[q_me] = HC[:, lanes(me)]

    for s in range(4):
        c = lax.rem(y + 1 + s, 4)
        SC[:, lanes(c, 512)] = (dot(hc, B[:, lanes(c, 512)], 1, 0) * inv_fan).astype(BF)
        for p in (4 * c, 4 * c + 1, 4 * c + 2, 4 * c + 3):
            @pl.when(p != me)
            def _(p=p):
                rcopy(S_X, SC.at[:, lanes(p)], SA.at[q_me], by_feat(p)).start()

    owe(S_X, SA.at[0:15])
    for piece in (2, 3):
        features_to(ahead, piece)
        features_to(behind, piece)
    owe(FX_X, FX.at[0:2])
    SA[q_me] = SC[:, lanes(me)]
    wait_recv(H_X, HT.at[0:15])
    ht = HT[...].reshape(256, 128)
    w2s, w2n = w2s_ref[...], w2n_ref[...]
    from_self = dot(w2s, ht, 1, 0)
    wait_recv(S_X, SA.at[0:15])

    sa = SA[...].reshape(256, 128)
    logits = from_self + dot(w2n, sa, 1, 0)
    top = jnp.max(logits, axis=0, keepdims=True)
    shifted = logits - top
    logprob = shifted - jnp.log(jnp.sum(jnp.exp(shifted), axis=0, keepdims=True))
    hot = lax.broadcasted_iota(jnp.int32, logits.shape, 0) == lab_ref[pl.ds(me, 1), :]
    picked = jnp.sum(jnp.where(hot, logprob, 0.0), axis=0, keepdims=True)
    weight = lw_ref[pl.ds(me, 1), :]
    chance = jnp.exp(picked)
    rest = 1.0 - chance
    slope = weight * (2.0 * rest * chance * picked - rest * rest)
    grad = (slope * (jnp.where(hot, 1.0, 0.0) - jnp.exp(logprob))).astype(BF)
    AGS[...] = dot(w2n, grad, 0, 0).astype(BF).reshape(16, 16, 128)
    send(AG_X, FEAT, lambda p: AGS.at[order(p)], AG.at[:, lanes(me)], by_feat, AGS.at[0:15])
    HOS[...] = dot(w2s, grad, 0, 0).astype(BF).reshape(16, 16, 128)
    send(HO_X, FEAT, lambda p: HOS.at[order(p)], HO.at[:, lanes(me)], by_feat, HOS.at[0:15])
    AG[:, lanes(me)] = AGS[q_me]
    HO[:, lanes(me)] = HOS[q_me]
    GT[0:grad.shape[0], :] = grad
    gt = GT[...]
    for part, table in enumerate((ht, sa)):
        second = dot(gt, table, 1, 1).astype(BF)
        for r in range(4):
            for c in range(2):
                GWS[4 * r + 2 * part + c] = second[64 * r:64 * r + 64, 128 * c:128 * c + 128]
    send(R1_X, FEAT, lambda p: GWS.at[p], GWR.at[me], by_feat, GWS.at[0:15])
    GWR[me] = GWS[me]
    LSS[0:1, :] = -rest * rest * picked * weight
    LSS[1:2, :] = weight
    send(L1_X, FEAT, lambda p: LSS, LSR.at[me], by_feat, LSR.at[0:15])
    LSR[me] = LSS[...]
    wait_recv(AG_X, AGS.at[0:15])
    ag = AG[...]
    for c in range(2):
        at = pl.ds(1024 * c, 1024)
        from_neigh = dot(ag, B[at, :], 1, 1) * inv_fan
        if c == 0:
            wait_recv(HO_X, HOS.at[0:15])
        PP[0, y, :, at] = jnp.where(FP[:, at] > 0, HO[:, at].astype(F32) + from_neigh, 0.0).astype(BF)
        piece = PP.at[0, y, :, at]
        for yp in YS:
            rcopy(PRE_X, piece, piece, by_y(yp)).start()
    owe(PRE_X, PP.at[0, 0:3])
    wait_recv(FX_X, FX.at[0:2])
    from_behind, from_ahead = FX.at[behind, :, 0:1024], FX.at[ahead, :, 1024:2048]
    rcopy(FY_X, from_behind, from_behind, by_x(ahead)).start()
    rcopy(FY_X, from_ahead, from_ahead, by_x(behind)).start()
    owe(FY_X, FX.at[0])
    wait_recv(R1_X, GWS.at[0:15])
    wait_recv(L1_X, LSR.at[0:15])
    rows = GWR[0].astype(F32)
    part = LSR[0]
    for p in range(1, 16):
        rows = rows + GWR[p].astype(F32)
        part = part + LSR[p]
    for t in range(8):
        T8[t] = rows[8 * t:8 * t + 8]
    L2S[...] = part
    send(R2_X, DP, lambda d: T8.at[lax.div(d, 2)], TR.at[md], by_dp, TR.at[0:15])
    send(L2_X, DP, lambda d: L2S, L2R.at[md], by_dp, L2R.at[0:15])
    TR[md] = T8[z]
    L2R[md] = part

    wait_recv(PRE_X, PP.at[0, 0:3])
    pre = PP[0].reshape(64, 2048)
    for c in range(4):
        at = pl.ds(512 * c, 512)
        PP[1, :, :, at] = (dot(pre, B[at, :], 1, 1) * inv_fan).astype(BF).reshape(4, 16, 512)
    wait_recv(R2_X, TR.at[0:15])
    AW[me, z] = jnp.sum(TR[...], axis=0).astype(BF)
    send(R3_X, ZS, lambda zp: AW.at[me, z], AW.at[me, z], by_z, AW.at[0, 0:7])

    wait_recv(FY_X, FX.at[0])
    full = dot(FX[...].reshape(256, 2048), PP[...].reshape(128, 2048), 1, 1)
    for d in range(16):
        for xs in range(4):
            GS[d, 4 * xs:4 * xs + 4, :] = full[64 * xs + 4 * d:64 * xs + 4 * d + 4, :].astype(BF)
    send(D_X, DP, lambda d: GS.at[d], GR.at[md], by_dp, GS.at[0:15])
    GR[md] = GS[md]

    wait_recv(R3_X, AW.at[0, 0:7])
    send(R4_X, FEAT, lambda p: AW.at[me], AW.at[me], by_feat, AW.at[0:15])
    wait_recv(L2_X, L2R.at[0:15])
    totals = jnp.sum(jnp.sum(L2R[...], axis=0), axis=1, keepdims=True)
    loss_total, norm_total = totals[0:1, :], totals[1:2, :]
    scale = 1.0 / norm_total
    loss_ref[...] = loss_total / norm_total

    wait_recv(D_X, GS.at[0:15])
    summed = GR[0].astype(F32)
    for d in range(1, 16):
        summed = summed + GR[d].astype(F32)
    summed = summed * scale
    for xs in range(4):
        RSS[xs, 0:4, :] = summed[4 * xs:4 * xs + 4, :]
    send(X_X, XS, lambda xp: RSS.at[xp], RX.at[x], by_x, RSS.at[0:3])
    RX[x] = RSS[x]
    wait_recv(R4_X, AW.at[0:15])
    classes = gw2_ref.shape[0]
    for p in range(16):
        for t in range(8):
            row = 64 * (p // 4) + 8 * t
            n = min(8, classes - row)
            if n > 0:
                gw2_ref[row:row + n, (p % 4) // 2, 128 * (p % 2):128 * (p % 2) + 128] = (
                    AW[p, t].astype(F32) * scale)[0:n]
    wait_recv(X_X, RSS.at[0:3])
    left = lax.broadcasted_iota(jnp.int32, (8, 128), 1) < 64
    for pair in range(2):
        a, b = RX[2 * pair], RX[2 * pair + 1]
        at = slice(128 * pair, 128 * pair + 128)
        gw1_ref[0, :, at] = jnp.where(left, a, pltpu.roll(b, 64, 1))[0:4]
        gw1_ref[1, :, at] = jnp.where(left, pltpu.roll(a, 64, 1), b)[0:4]
    for wait in drains:
        wait()


def on_device(features, neighbors, labels, loss_weight, w1_self, w1_neigh, w2_self, w2_neigh):
    fan = neighbors.shape[1]
    vmem = pl.BlockSpec(memory_space=pltpu.VMEM)
    hbm = pl.BlockSpec(memory_space=pltpu.HBM)
    S = pltpu.VMEM
    loss, grad_w1, grad_w2 = pl.pallas_call(
        functools.partial(kernel, fan),
        out_shape=(
            jax.ShapeDtypeStruct((1, 1), F32),
            jax.ShapeDtypeStruct((2, 4, 256), F32),
            jax.ShapeDtypeStruct((w2_self.shape[1], 2, 256), F32),
        ),
        in_specs=[hbm] * 8,
        out_specs=(vmem, vmem, vmem),
        scratch_shapes=[
            S((2048, 2048), BF),
            S((4, 64, 2048), BF),
            S((16, 64, 128), BF),
            S((2, 4, 4, 64, 256), BF),
            S((16, 16, 128), F32),
            S((16, 16, 128), BF),
            S((16, 2048), F32),
            S((16, 2048), BF),
            S((16, 2048), F32),
            S((16, 2048), BF),
            S((16, 2048), BF),
            S((16, 16, 128), BF),
            S((16, 16, 128), BF),
            S((256, 128), BF),
            S((16, 16, 128), BF),
            S((16, 16, 128), BF),
            S((16, 2048), BF),
            S((16, 2048), BF),
            S((2, 4, 16, 2048), BF),
            S((16, 16, 128), BF),
            S((16, 16, 128), BF),
            S((4, 8, 128), F32),
            S((4, 8, 128), F32),
            S((16, 64, 128), BF),
            S((16, 64, 128), BF),
            S((8, 128), F32),
            S((16, 8, 128), F32),
            S((8, 8, 128), F32),
            S((16, 8, 128), F32),
            S((8, 128), F32),
            S((16, 8, 128), F32),
            S((16, 8, 8, 128), BF),
            S((fan, 2048), jnp.int32),
            S((16, 128), jnp.int32),
            S((16, 128), F32),
            S(w2_self.shape[::-1], BF),
            S(w2_neigh.shape[::-1], BF),
            pltpu.SemaphoreType.DMA((2, 23)),
            pltpu.SemaphoreType.DMA((7,)),
        ],
        compiler_params=pltpu.CompilerParams(
            collective_id=0, has_side_effects=True, vmem_limit_bytes=40 * 2 ** 20),
        name="sage_step",
    )(*(pltpu.with_memory_space_constraint(a, pltpu.HBM) for a in (
        features, neighbors.T, labels.reshape(16, 128), loss_weight.reshape(16, 128),
        w1_self, w1_neigh, w2_self.T, w2_neigh.T)))
    return loss.reshape(()), grad_w1, grad_w2.transpose(1, 2, 0)


def solution(mesh):
    in_specs = (
        P("feat", "dp"),
        P("dp", None),
        P("dp"),
        P("dp"),
        P("feat", None),
        P("feat", None),
        P(),
        P(),
    )
    out_specs = (P(), P(None, ("feat", "dp"), None), P())
    return jax.shard_map(
        on_device, mesh=mesh, in_specs=in_specs, out_specs=out_specs, check_vma=False
    )
```

```python
import functools

import jax
import jax.numpy as jnp
from jax import lax
from jax.experimental import pallas as pl
from jax.experimental.pallas import tpu as pltpu
from jax.sharding import PartitionSpec as P

BF = jnp.bfloat16
F32 = jnp.float32

(WA_X, WB_X, WC_X, WD_X, WE_X, WF_X, FWD_X, F_X, PS_X, PN_X, H_X, S_X, HO_X, AG_X, PRE_X, FX_X, FY_X,
 D_X, X_X, R1_X, L1_X, R2_X, L2_X, R3_X, R4_X) = range(25)


def dot(a, b, ca, cb):
    return lax.dot_general(a, b, (((ca,), (cb,)), ((), ())), preferred_element_type=F32)


def lanes(p, width=128):
    return pl.ds(pl.multiple_of(p * width, width), width)


def kernel(fan, f_hbm, nbr_hbm, lab_hbm, lw_hbm, ws_hbm, wn_hbm, w2s_hbm, w2n_hbm,
           loss_ref, gw1_ref, gw2_ref,
           B, FX, FO, WG, PSS, PNS, PS, PN, FP, HC, SC, HT, SA, GT, HOS, AGS, HO, AG,
           PP, GS, GR, RSS, RX, GWS, GWR, LSS, LSR, T8, TR, L2S, L2R, AW,
           nbr_ref, lab_ref, lw_ref, w2s_ref, w2n_ref, sems, lsem):
    me, md = lax.axis_index("feat"), lax.axis_index("dp")
    x, y = lax.rem(me, 4), lax.div(me, 4)
    core, z = lax.rem(md, 2), lax.div(md, 2)
    mate = (me, md + 1 - 2 * core)
    inv_fan = 1.0 / fan

    def order(p):
        return lax.rem(p, 4) * 4 + lax.div(p, 4)

    q_me = order(me)

    near = lambda d, n: min(d, n - d)
    XS = [lax.rem(x + d, 4) for d in (2, 1, 3)]
    YS = [lax.rem(y + d, 4) for d in (2, 1, 3)]
    ZS = [lax.rem(z + d, 8) for d in (4, 3, 5, 2, 6, 1, 7)]
    plane = sorted(((a, b) for a in range(4) for b in range(4) if a or b),
                   key=lambda o: -near(o[0], 4) - near(o[1], 4))
    FEAT = [lax.rem(y + a, 4) * 4 + lax.rem(x + b, 4) for a, b in plane]
    line = sorted(((a, b) for a in range(8) for b in range(2) if a or b),
                  key=lambda o: -near(o[0], 8))
    DP = [lax.rem(z + a, 8) * 2 + (core if b == 0 else 1 - core) for a, b in line]

    def rcopy(row, src, dst, dev):
        return pltpu.make_async_remote_copy(
            src_ref=src, dst_ref=dst, send_sem=sems.at[0, row], recv_sem=sems.at[1, row],
            device_id=dev, device_id_type=pl.DeviceIdType.MESH)

    by_feat = lambda p: (p, md)
    by_dp = lambda d: (me, d)
    by_x = lambda xp: (y * 4 + xp, md)
    by_y = lambda yp: (yp * 4 + x, md)
    by_z = lambda zp: (me, zp * 2 + core)
    drains = []

    def owe(row, view):
        drains.append(lambda: rcopy(row, view, view, mate).wait_send())

    def send(row, peers, src, dst, dev, view):
        for p in peers:
            rcopy(row, src(p), dst, dev(p)).start()
        owe(row, view)

    def wait_recv(row, view):
        rcopy(row, view, view, mate).wait_recv()

    bar = pltpu.get_barrier_semaphore()
    mesh_id = pl.DeviceIdType.MESH
    for p in FEAT:
        pl.semaphore_signal(bar, 1, device_id=by_feat(p), device_id_type=mesh_id)
    for d in DP:
        pl.semaphore_signal(bar, 1, device_id=by_dp(d), device_id_type=mesh_id)

    local = [
        pltpu.make_async_copy(f_hbm, FX.at[x], lsem.at[1]),
        pltpu.make_async_copy(nbr_hbm, nbr_ref, lsem.at[2]),
        pltpu.make_async_copy(lab_hbm, lab_ref, lsem.at[3]),
        pltpu.make_async_copy(lw_hbm, lw_ref, lsem.at[4]),
        pltpu.make_async_copy(w2s_hbm, w2s_ref, lsem.at[5]),
        pltpu.make_async_copy(w2n_hbm, w2n_ref, lsem.at[6]),
    ]
    own_w = pltpu.make_async_copy(ws_hbm, WG.at[core, y, x], lsem.at[0])

    @pl.when(core == 0)
    def _():
        own_w.start()

    @pl.when(core == 1)
    def _():
        pltpu.make_async_copy(wn_hbm, WG.at[core, y, x], lsem.at[0]).start()

    for c in local:
        c.start()
    own_w.wait()
    local[0].wait()
    pl.semaphore_wait(bar, 30)

    upper, lower = WG.at[core, y, x, 0:32], WG.at[core, y, x, 32:64]
    send(WA_X, XS, lambda xp: upper, upper, by_x, WG.at[0, 0, 0:3, 0:32])
    send(WB_X, YS, lambda yp: lower, lower, by_y, WG.at[0, 0, 0:3, 32:64])
    send(F_X, FEAT, lambda p: FX.at[x, :, lanes(p)], FO.at[me], by_feat, FO.at[0:15])
    for c in local[1:]:
        c.wait()
    FO[me] = FX[x, :, lanes(me)]
    GT[...] = jnp.zeros_like(GT)
    RSS[...] = jnp.zeros_like(RSS)
    LSS[...] = jnp.zeros_like(LSS)

    iota = lax.broadcasted_iota(jnp.int32, (256, 128), 0).astype(F32).astype(BF).reshape(16, 16, 128)

    def spread(row):
        return jnp.broadcast_to(row.astype(F32), (16, 128)).astype(BF)

    def build(t, carry):
        lo = lanes(t)
        ids = nbr_ref[:, lo]
        times = jnp.zeros((fan, 128), F32)
        for k in range(fan):
            times = times + jnp.where(ids == ids[k:k + 1], 1.0, 0.0)
        count = [spread(times[k:k + 1]) for k in range(fan)]
        low = [spread(ids[k:k + 1] & 255) for k in range(fan)]
        high = [spread(ids[k:k + 1] >> 8) for k in range(fan)]

        def group(g, inner):
            here = jnp.full((16, 128), g, jnp.int32).astype(F32).astype(BF)
            acc = jnp.zeros((16, 16, 128), BF)
            for k in range(fan):
                at = jnp.where(high[k] == here, low[k], BF(300))
                acc = jnp.where(iota == at[None], count[k][None], acc)
            B[lanes(g, 256), lo] = acc.reshape(256, 128)
            return inner

        return lax.fori_loop(0, 8, group, carry)

    lax.fori_loop(0, 6, build, 0)
    wait_recv(WA_X, WG.at[0, 0, 0:3, 0:32])
    wait_recv(WB_X, WG.at[0, 0, 0:3, 32:64])

    def hand_over(ready):
        rcopy(FWD_X, ready, ready, mate).start()

    (yo, ya, yb), (xo, xa, xb) = YS, XS
    uppers, lowers = WG.at[core, y, :, 0:32], WG.at[core, :, x, 32:64]
    send(WC_X, (ya, yb), lambda yp: uppers, uppers, by_y, WG.at[0, 0:2, :, 0:32])
    send(WD_X, (xa, xb), lambda xp: lowers, lowers, by_x, WG.at[0, :, 0:2, 32:64])
    hand_over(uppers)
    hand_over(lowers)
    lax.fori_loop(6, 14, build, 0)
    wait_recv(WC_X, WG.at[0, 0:2, :, 0:32])
    first_half, second_half = WG.at[core, yb, 0:2, 0:32], WG.at[core, ya, 2:4, 0:32]
    rcopy(WE_X, first_half, first_half, by_y(ya)).start()
    rcopy(WE_X, second_half, second_half, by_y(yb)).start()
    owe(WE_X, WG.at[0, 0, :, 0:32])
    wait_recv(WD_X, WG.at[0, :, 0:2, 32:64])
    first_half, second_half = WG.at[core, 0:2, xb, 32:64], WG.at[core, 2:4, xa, 32:64]
    rcopy(WF_X, first_half, first_half, by_x(xa)).start()
    rcopy(WF_X, second_half, second_half, by_x(xb)).start()
    owe(WF_X, WG.at[0, :, 0, 32:64])
    for yp in (ya, yb):
        hand_over(WG.at[core, yp, :, 0:32])
    for xp in (xa, xb):
        hand_over(WG.at[core, :, xp, 32:64])
    lax.fori_loop(14, 16, build, 0)
    wait_recv(WE_X, WG.at[0, 0, :, 0:32])
    hand_over(WG.at[core, yo, :, 0:32])
    wait_recv(WF_X, WG.at[0, :, 0, 32:64])
    hand_over(WG.at[core, :, xo, 32:64])
    owe(FWD_X, WG.at[0])
    wait_recv(F_X, FO.at[0:15])
    wait_recv(FWD_X, WG.at[0])

    fo = FO[...].reshape(1024, 128)
    PNS[...] = dot(WG[1].reshape(1024, 256), fo, 0, 0).astype(BF).reshape(16, 16, 128)
    send(PN_X, FEAT, lambda p: PNS.at[order(p)], PN.at[:, lanes(me)], by_feat, PNS.at[0:15])
    PSS[...] = dot(WG[0].reshape(1024, 256), fo, 0, 0).reshape(16, 16, 128)
    send(PS_X, FEAT, lambda p: PSS.at[order(p)], PS.at[:, lanes(me)], by_feat, PSS.at[0:15])
    PN[:, lanes(me)] = PNS[q_me]
    PS[:, lanes(me)] = PSS[q_me]

    def features_to(xp, piece):
        part = FX.at[x, :, lanes(piece, 512)]
        rcopy(FX_X, part, part, by_x(xp)).start()

    ahead, behind = lax.rem(x + 1, 4), lax.rem(x + 3, 4)
    features_to(ahead, 0)
    features_to(behind, 0)
    wait_recv(PN_X, PNS.at[0:15])
    features_to(ahead, 1)
    features_to(behind, 1)
    mean = dot(PN[...], B[...], 1, 0) * inv_fan
    wait_recv(PS_X, PSS.at[0:15])
    first = PS[...] + mean
    FP[...] = first
    hc = jnp.maximum(first, 0.0).astype(BF)
    HC[...] = hc
    send(H_X, FEAT, lambda p: HC.at[:, lanes(p)], HT.at[q_me], by_feat, HT.at[0:15])
    HT[q_me] = HC[:, lanes(me)]

    for s in range(4):
        c = lax.rem(y + 1 + s, 4)
        SC[:, lanes(c, 512)] = (dot(hc, B[:, lanes(c, 512)], 1, 0) * inv_fan).astype(BF)
        for p in (4 * c, 4 * c + 1, 4 * c + 2, 4 * c + 3):
            @pl.when(p != me)
            def _(p=p):
                rcopy(S_X, SC.at[:, lanes(p)], SA.at[q_me], by_feat(p)).start()

    owe(S_X, SA.at[0:15])
    for piece in (2, 3):
        features_to(ahead, piece)
        features_to(behind, piece)
    owe(FX_X, FX.at[0:2])
    SA[q_me] = SC[:, lanes(me)]
    wait_recv(H_X, HT.at[0:15])
    ht = HT[...].reshape(256, 128)
    w2s, w2n = w2s_ref[...], w2n_ref[...]
    from_self = dot(w2s, ht, 1, 0)
    wait_recv(S_X, SA.at[0:15])

    sa = SA[...].reshape(256, 128)
    logits = from_self + dot(w2n, sa, 1, 0)
    top = jnp.max(logits, axis=0, keepdims=True)
    shifted = logits - top
    logprob = shifted - jnp.log(jnp.sum(jnp.exp(shifted), axis=0, keepdims=True))
    hot = lax.broadcasted_iota(jnp.int32, logits.shape, 0) == lab_ref[pl.ds(me, 1), :]
    picked = jnp.sum(jnp.where(hot, logprob, 0.0), axis=0, keepdims=True)
    weight = lw_ref[pl.ds(me, 1), :]
    chance = jnp.exp(picked)
    rest = 1.0 - chance
    slope = weight * (2.0 * rest * chance * picked - rest * rest)
    grad = (slope * (jnp.where(hot, 1.0, 0.0) - jnp.exp(logprob))).astype(BF)
    AGS[...] = dot(w2n, grad, 0, 0).astype(BF).reshape(16, 16, 128)
    send(AG_X, FEAT, lambda p: AGS.at[order(p)], AG.at[:, lanes(me)], by_feat, AGS.at[0:15])
    HOS[...] = dot(w2s, grad, 0, 0).astype(BF).reshape(16, 16, 128)
    send(HO_X, FEAT, lambda p: HOS.at[order(p)], HO.at[:, lanes(me)], by_feat, HOS.at[0:15])
    AG[:, lanes(me)] = AGS[q_me]
    HO[:, lanes(me)] = HOS[q_me]
    GT[0:grad.shape[0], :] = grad
    gt = GT[...]
    for part, table in enumerate((ht, sa)):
        second = dot(gt, table, 1, 1).astype(BF)
        for r in range(4):
            for c in range(2):
                GWS[4 * r + 2 * part + c] = second[64 * r:64 * r + 64, 128 * c:128 * c + 128]
    send(R1_X, FEAT, lambda p: GWS.at[p], GWR.at[me], by_feat, GWS.at[0:15])
    GWR[me] = GWS[me]
    LSS[0:1, :] = -rest * rest * picked * weight
    LSS[1:2, :] = weight
    send(L1_X, FEAT, lambda p: LSS, LSR.at[me], by_feat, LSR.at[0:15])
    LSR[me] = LSS[...]
    wait_recv(AG_X, AGS.at[0:15])
    ag = AG[...]
    for c in range(2):
        at = pl.ds(1024 * c, 1024)
        from_neigh = dot(ag, B[at, :], 1, 1) * inv_fan
        if c == 0:
            wait_recv(HO_X, HOS.at[0:15])
        PP[0, y, :, at] = jnp.where(FP[:, at] > 0, HO[:, at].astype(F32) + from_neigh, 0.0).astype(BF)
        piece = PP.at[0, y, :, at]
        for yp in YS:
            rcopy(PRE_X, piece, piece, by_y(yp)).start()
    owe(PRE_X, PP.at[0, 0:3])
    wait_recv(FX_X, FX.at[0:2])
    from_behind, from_ahead = FX.at[behind, :, 0:1024], FX.at[ahead, :, 1024:2048]
    rcopy(FY_X, from_behind, from_behind, by_x(ahead)).start()
    rcopy(FY_X, from_ahead, from_ahead, by_x(behind)).start()
    owe(FY_X, FX.at[0])
    wait_recv(R1_X, GWS.at[0:15])
    wait_recv(L1_X, LSR.at[0:15])
    rows = GWR[0].astype(F32)
    part = LSR[0]
    for p in range(1, 16):
        rows = rows + GWR[p].astype(F32)
        part = part + LSR[p]
    for t in range(8):
        T8[t] = rows[8 * t:8 * t + 8]
    L2S[...] = part
    send(R2_X, DP, lambda d: T8.at[lax.div(d, 2)], TR.at[md], by_dp, TR.at[0:15])
    send(L2_X, DP, lambda d: L2S, L2R.at[md], by_dp, L2R.at[0:15])
    TR[md] = T8[z]
    L2R[md] = part

    wait_recv(PRE_X, PP.at[0, 0:3])
    pre = PP[0].reshape(64, 2048)
    for c in range(4):
        at = pl.ds(512 * c, 512)
        PP[1, :, :, at] = (dot(pre, B[at, :], 1, 1) * inv_fan).astype(BF).reshape(4, 16, 512)
    wait_recv(R2_X, TR.at[0:15])
    AW[me, z] = jnp.sum(TR[...], axis=0).astype(BF)
    send(R3_X, ZS, lambda zp: AW.at[me, z], AW.at[me, z], by_z, AW.at[0, 0:7])

    wait_recv(FY_X, FX.at[0])
    full = dot(FX[...].reshape(256, 2048), PP[...].reshape(128, 2048), 1, 1)
    for d in range(16):
        for xs in range(4):
            GS[d, 4 * xs:4 * xs + 4, :] = full[64 * xs + 4 * d:64 * xs + 4 * d + 4, :].astype(BF)
    send(D_X, DP, lambda d: GS.at[d], GR.at[md], by_dp, GS.at[0:15])
    GR[md] = GS[md]

    wait_recv(R3_X, AW.at[0, 0:7])
    send(R4_X, FEAT, lambda p: AW.at[me], AW.at[me], by_feat, AW.at[0:15])
    wait_recv(L2_X, L2R.at[0:15])
    totals = jnp.sum(jnp.sum(L2R[...], axis=0), axis=1, keepdims=True)
    loss_total, norm_total = totals[0:1, :], totals[1:2, :]
    scale = 1.0 / norm_total
    loss_ref[...] = loss_total / norm_total

    wait_recv(D_X, GS.at[0:15])
    summed = GR[0].astype(F32)
    for d in range(1, 16):
        summed = summed + GR[d].astype(F32)
    summed = summed * scale
    for xs in range(4):
        RSS[xs, 0:4, :] = summed[4 * xs:4 * xs + 4, :]
    send(X_X, XS, lambda xp: RSS.at[xp], RX.at[x], by_x, RSS.at[0:3])
    RX[x] = RSS[x]
    wait_recv(R4_X, AW.at[0:15])
    classes = gw2_ref.shape[0]
    for p in range(16):
        for t in range(8):
            row = 64 * (p // 4) + 8 * t
            n = min(8, classes - row)
            if n > 0:
                gw2_ref[row:row + n, (p % 4) // 2, 128 * (p % 2):128 * (p % 2) + 128] = (
                    AW[p, t].astype(F32) * scale)[0:n]
    wait_recv(X_X, RSS.at[0:3])
    left = lax.broadcasted_iota(jnp.int32, (8, 128), 1) < 64
    for pair in range(2):
        a, b = RX[2 * pair], RX[2 * pair + 1]
        at = slice(128 * pair, 128 * pair + 128)
        gw1_ref[0, :, at] = jnp.where(left, a, pltpu.roll(b, 64, 1))[0:4]
        gw1_ref[1, :, at] = jnp.where(left, pltpu.roll(a, 64, 1), b)[0:4]
    for wait in drains:
        wait()


def on_device(features, neighbors, labels, loss_weight, w1_self, w1_neigh, w2_self, w2_neigh):
    fan = neighbors.shape[1]
    vmem = pl.BlockSpec(memory_space=pltpu.VMEM)
    hbm = pl.BlockSpec(memory_space=pltpu.HBM)
    S = pltpu.VMEM
    loss, grad_w1, grad_w2 = pl.pallas_call(
        functools.partial(kernel, fan),
        out_shape=(
            jax.ShapeDtypeStruct((1, 1), F32),
            jax.ShapeDtypeStruct((2, 4, 256), F32),
            jax.ShapeDtypeStruct((w2_self.shape[1], 2, 256), F32),
        ),
        in_specs=[hbm] * 8,
        out_specs=(vmem, vmem, vmem),
        scratch_shapes=[
            S((2048, 2048), BF),
            S((4, 64, 2048), BF),
            S((16, 64, 128), BF),
            S((2, 4, 4, 64, 256), BF),
            S((16, 16, 128), F32),
            S((16, 16, 128), BF),
            S((16, 2048), F32),
            S((16, 2048), BF),
            S((16, 2048), F32),
            S((16, 2048), BF),
            S((16, 2048), BF),
            S((16, 16, 128), BF),
            S((16, 16, 128), BF),
            S((256, 128), BF),
            S((16, 16, 128), BF),
            S((16, 16, 128), BF),
            S((16, 2048), BF),
            S((16, 2048), BF),
            S((2, 4, 16, 2048), BF),
            S((16, 16, 128), BF),
            S((16, 16, 128), BF),
            S((4, 8, 128), F32),
            S((4, 8, 128), F32),
            S((16, 64, 128), BF),
            S((16, 64, 128), BF),
            S((8, 128), F32),
            S((16, 8, 128), F32),
            S((8, 8, 128), F32),
            S((16, 8, 128), F32),
            S((8, 128), F32),
            S((16, 8, 128), F32),
            S((16, 8, 8, 128), BF),
            S((fan, 2048), jnp.int32),
            S((16, 128), jnp.int32),
            S((16, 128), F32),
            S(w2_self.shape[::-1], BF),
            S(w2_neigh.shape[::-1], BF),
            pltpu.SemaphoreType.DMA((2, 25)),
            pltpu.SemaphoreType.DMA((7,)),
        ],
        compiler_params=pltpu.CompilerParams(
            collective_id=0, has_side_effects=True, vmem_limit_bytes=40 * 2 ** 20),
        name="sage_step",
    )(*(pltpu.with_memory_space_constraint(a, pltpu.HBM) for a in (
        features, neighbors.T, labels.reshape(16, 128), loss_weight.reshape(16, 128),
        w1_self, w1_neigh, w2_self.T, w2_neigh.T)))
    return loss.reshape(()), grad_w1, grad_w2.transpose(1, 2, 0)


def solution(mesh):
    in_specs = (
        P("feat", "dp"),
        P("dp", None),
        P("dp"),
        P("dp"),
        P("feat", None),
        P("feat", None),
        P(),
        P(),
    )
    out_specs = (P(), P(None, ("feat", "dp"), None), P())
    return jax.shard_map(
        on_device, mesh=mesh, in_specs=in_specs, out_specs=out_specs, check_vma=False
    )
```

```python
import functools

import jax
import jax.numpy as jnp
from jax import lax
from jax.experimental import pallas as pl
from jax.experimental.pallas import tpu as pltpu
from jax.sharding import PartitionSpec as P

BF = jnp.bfloat16
F32 = jnp.float32

(WA_X, WB_X, WC_X, WD_X, FWD_X, F_X, PS_X, PN_X, H_X, S_X, HO_X, AG_X, PRE_X, FX_X, FY_X,
 D_X, X_X, R1_X, L1_X, R2_X, L2_X, R3_X, R4_X) = range(23)


def dot(a, b, ca, cb):
    return lax.dot_general(a, b, (((ca,), (cb,)), ((), ())), preferred_element_type=F32)


def lanes(p, width=128):
    return pl.ds(pl.multiple_of(p * width, width), width)


def kernel(fan, f_hbm, nbr_hbm, lab_hbm, lw_hbm, ws_hbm, wn_hbm, w2s_hbm, w2n_hbm,
           loss_ref, gw1_ref, gw2_ref,
           B, FX, FO, WG, PSS, PNS, PS, PN, FP, HC, SC, HT, SA, GT, HOS, AGS, HO, AG,
           PP, GS, GR, RSS, RX, GWS, GWR, LSS, LSR, T8, TR, L2S, L2R, AW,
           nbr_ref, lab_ref, lw_ref, w2s_ref, w2n_ref, sems, lsem):
    me, md = lax.axis_index("feat"), lax.axis_index("dp")
    x, y = lax.rem(me, 4), lax.div(me, 4)
    core, z = lax.rem(md, 2), lax.div(md, 2)
    mate = (me, md + 1 - 2 * core)
    inv_fan = 1.0 / fan

    def order(p):
        return lax.rem(p, 4) * 4 + lax.div(p, 4)

    q_me = order(me)

    near = lambda d, n: min(d, n - d)
    XS = [lax.rem(x + d, 4) for d in (2, 1, 3)]
    YS = [lax.rem(y + d, 4) for d in (2, 1, 3)]
    ZS = [lax.rem(z + d, 8) for d in (4, 3, 5, 2, 6, 1, 7)]
    plane = sorted(((a, b) for a in range(4) for b in range(4) if a or b),
                   key=lambda o: -near(o[0], 4) - near(o[1], 4))
    FEAT = [lax.rem(y + a, 4) * 4 + lax.rem(x + b, 4) for a, b in plane]
    line = sorted(((a, b) for a in range(8) for b in range(2) if a or b),
                  key=lambda o: -near(o[0], 8))
    DP = [lax.rem(z + a, 8) * 2 + (core if b == 0 else 1 - core) for a, b in line]

    def rcopy(row, src, dst, dev):
        return pltpu.make_async_remote_copy(
            src_ref=src, dst_ref=dst, send_sem=sems.at[0, row], recv_sem=sems.at[1, row],
            device_id=dev, device_id_type=pl.DeviceIdType.MESH)

    by_feat = lambda p: (p, md)
    by_dp = lambda d: (me, d)
    by_x = lambda xp: (y * 4 + xp, md)
    by_y = lambda yp: (yp * 4 + x, md)
    by_z = lambda zp: (me, zp * 2 + core)
    drains = []

    def owe(row, view):
        drains.append(lambda: rcopy(row, view, view, mate).wait_send())

    def send(row, peers, src, dst, dev, view):
        for p in peers:
            rcopy(row, src(p), dst, dev(p)).start()
        owe(row, view)

    def wait_recv(row, view):
        rcopy(row, view, view, mate).wait_recv()

    bar = pltpu.get_barrier_semaphore()
    mesh_id = pl.DeviceIdType.MESH
    for p in FEAT:
        pl.semaphore_signal(bar, 1, device_id=by_feat(p), device_id_type=mesh_id)
    for d in DP:
        pl.semaphore_signal(bar, 1, device_id=by_dp(d), device_id_type=mesh_id)

    local = [
        pltpu.make_async_copy(f_hbm, FX.at[x], lsem.at[1]),
        pltpu.make_async_copy(nbr_hbm, nbr_ref, lsem.at[2]),
        pltpu.make_async_copy(lab_hbm, lab_ref, lsem.at[3]),
        pltpu.make_async_copy(lw_hbm, lw_ref, lsem.at[4]),
        pltpu.make_async_copy(w2s_hbm, w2s_ref, lsem.at[5]),
        pltpu.make_async_copy(w2n_hbm, w2n_ref, lsem.at[6]),
    ]
    own_w = pltpu.make_async_copy(ws_hbm, WG.at[core, y, x], lsem.at[0])

    @pl.when(core == 0)
    def _():
        own_w.start()

    @pl.when(core == 1)
    def _():
        pltpu.make_async_copy(wn_hbm, WG.at[core, y, x], lsem.at[0]).start()

    for c in local:
        c.start()
    own_w.wait()
    local[0].wait()
    pl.semaphore_wait(bar, 30)

    upper, lower = WG.at[core, y, x, 0:32], WG.at[core, y, x, 32:64]
    send(WA_X, XS, lambda xp: upper, upper, by_x, WG.at[0, 0, 0:3, 0:32])
    send(WB_X, YS, lambda yp: lower, lower, by_y, WG.at[0, 0, 0:3, 32:64])

    def features_of(p):
        rcopy(F_X, FX.at[x, :, lanes(p)], FO.at[me], by_feat(p)).start()

    for p in FEAT[:6]:
        features_of(p)
    for c in local[1:]:
        c.wait()
    FO[me] = FX[x, :, lanes(me)]
    GT[...] = jnp.zeros_like(GT)
    RSS[...] = jnp.zeros_like(RSS)
    LSS[...] = jnp.zeros_like(LSS)

    iota = lax.broadcasted_iota(jnp.int32, (256, 128), 0).astype(F32).astype(BF).reshape(16, 16, 128)

    def spread(row):
        return jnp.broadcast_to(row.astype(F32), (16, 128)).astype(BF)

    def build(t, carry):
        lo = lanes(t)
        ids = nbr_ref[:, lo]
        times = jnp.zeros((fan, 128), F32)
        for k in range(fan):
            times = times + jnp.where(ids == ids[k:k + 1], 1.0, 0.0)
        count = [spread(times[k:k + 1]) for k in range(fan)]
        low = [spread(ids[k:k + 1] & 255) for k in range(fan)]
        high = [spread(ids[k:k + 1] >> 8) for k in range(fan)]

        def group(g, inner):
            here = jnp.full((16, 128), g, jnp.int32).astype(F32).astype(BF)
            acc = jnp.zeros((16, 16, 128), BF)
            for k in range(fan):
                at = jnp.where(high[k] == here, low[k], BF(300))
                acc = jnp.where(iota == at[None], count[k][None], acc)
            B[lanes(g, 256), lo] = acc.reshape(256, 128)
            return inner

        return lax.fori_loop(0, 8, group, carry)

    lax.fori_loop(0, 4, build, 0)
    wait_recv(WA_X, WG.at[0, 0, 0:3, 0:32])
    wait_recv(WB_X, WG.at[0, 0, 0:3, 32:64])
    uppers, lowers = WG.at[core, y, :, 0:32], WG.at[core, :, x, 32:64]
    send(WC_X, YS, lambda yp: uppers, uppers, by_y, WG.at[0, 0:3, :, 0:32])
    send(WD_X, XS, lambda xp: lowers, lowers, by_x, WG.at[0, :, 0:3, 32:64])
    for ready in (uppers, lowers):
        rcopy(FWD_X, ready, ready, mate).start()
    for p in FEAT[6:]:
        features_of(p)
    owe(F_X, FO.at[0:15])
    lax.fori_loop(4, 13, build, 0)
    wait_recv(WC_X, WG.at[0, 0:3, :, 0:32])
    for yp in YS:
        ready = WG.at[core, yp, :, 0:32]
        rcopy(FWD_X, ready, ready, mate).start()
    wait_recv(WD_X, WG.at[0, :, 0:3, 32:64])
    for xp in XS:
        ready = WG.at[core, :, xp, 32:64]
        rcopy(FWD_X, ready, ready, mate).start()
    owe(FWD_X, WG.at[0])
    lax.fori_loop(13, 16, build, 0)
    wait_recv(F_X, FO.at[0:15])
    wait_recv(FWD_X, WG.at[0])

    fo = FO[...].reshape(1024, 128)
    PNS[...] = dot(WG[1].reshape(1024, 256), fo, 0, 0).astype(BF).reshape(16, 16, 128)
    send(PN_X, FEAT, lambda p: PNS.at[order(p)], PN.at[:, lanes(me)], by_feat, PNS.at[0:15])
    PSS[...] = dot(WG[0].reshape(1024, 256), fo, 0, 0).reshape(16, 16, 128)
    send(PS_X, FEAT, lambda p: PSS.at[order(p)], PS.at[:, lanes(me)], by_feat, PSS.at[0:15])
    PN[:, lanes(me)] = PNS[q_me]
    PS[:, lanes(me)] = PSS[q_me]

    def features_to(xp, piece):
        part = FX.at[x, :, lanes(piece, 512)]
        rcopy(FX_X, part, part, by_x(xp)).start()

    ahead, behind = lax.rem(x + 1, 4), lax.rem(x + 3, 4)
    features_to(ahead, 0)
    features_to(behind, 0)
    wait_recv(PN_X, PNS.at[0:15])
    features_to(ahead, 1)
    features_to(behind, 1)
    mean = dot(PN[...], B[...], 1, 0) * inv_fan
    wait_recv(PS_X, PSS.at[0:15])
    first = PS[...] + mean
    FP[...] = first
    hc = jnp.maximum(first, 0.0).astype(BF)
    HC[...] = hc
    send(H_X, FEAT, lambda p: HC.at[:, lanes(p)], HT.at[q_me], by_feat, HT.at[0:15])
    HT[q_me] = HC[:, lanes(me)]

    for s in range(4):
        c = lax.rem(y + 1 + s, 4)
        SC[:, lanes(c, 512)] = (dot(hc, B[:, lanes(c, 512)], 1, 0) * inv_fan).astype(BF)
        for p in (4 * c, 4 * c + 1, 4 * c + 2, 4 * c + 3):
            @pl.when(p != me)
            def _(p=p):
                rcopy(S_X, SC.at[:, lanes(p)], SA.at[q_me], by_feat(p)).start()

    owe(S_X, SA.at[0:15])
    for piece in (2, 3):
        features_to(ahead, piece)
        features_to(behind, piece)
    owe(FX_X, FX.at[0:2])
    SA[q_me] = SC[:, lanes(me)]
    wait_recv(H_X, HT.at[0:15])
    ht = HT[...].reshape(256, 128)
    w2s, w2n = w2s_ref[...], w2n_ref[...]
    from_self = dot(w2s, ht, 1, 0)
    wait_recv(S_X, SA.at[0:15])

    sa = SA[...].reshape(256, 128)
    logits = from_self + dot(w2n, sa, 1, 0)
    top = jnp.max(logits, axis=0, keepdims=True)
    shifted = logits - top
    logprob = shifted - jnp.log(jnp.sum(jnp.exp(shifted), axis=0, keepdims=True))
    hot = lax.broadcasted_iota(jnp.int32, logits.shape, 0) == lab_ref[pl.ds(me, 1), :]
    picked = jnp.sum(jnp.where(hot, logprob, 0.0), axis=0, keepdims=True)
    weight = lw_ref[pl.ds(me, 1), :]
    chance = jnp.exp(picked)
    rest = 1.0 - chance
    slope = weight * (2.0 * rest * chance * picked - rest * rest)
    grad = (slope * (jnp.where(hot, 1.0, 0.0) - jnp.exp(logprob))).astype(BF)
    AGS[...] = dot(w2n, grad, 0, 0).astype(BF).reshape(16, 16, 128)
    send(AG_X, FEAT, lambda p: AGS.at[order(p)], AG.at[:, lanes(me)], by_feat, AGS.at[0:15])
    HOS[...] = dot(w2s, grad, 0, 0).astype(BF).reshape(16, 16, 128)
    send(HO_X, FEAT, lambda p: HOS.at[order(p)], HO.at[:, lanes(me)], by_feat, HOS.at[0:15])
    AG[:, lanes(me)] = AGS[q_me]
    HO[:, lanes(me)] = HOS[q_me]
    GT[0:grad.shape[0], :] = grad
    gt = GT[...]
    for part, table in enumerate((ht, sa)):
        second = dot(gt, table, 1, 1).astype(BF)
        for r in range(4):
            for c in range(2):
                GWS[4 * r + 2 * part + c] = second[64 * r:64 * r + 64, 128 * c:128 * c + 128]
    send(R1_X, FEAT, lambda p: GWS.at[p], GWR.at[me], by_feat, GWS.at[0:15])
    GWR[me] = GWS[me]
    LSS[0:1, :] = -rest * rest * picked * weight
    LSS[1:2, :] = weight
    send(L1_X, FEAT, lambda p: LSS, LSR.at[me], by_feat, LSR.at[0:15])
    LSR[me] = LSS[...]
    wait_recv(AG_X, AGS.at[0:15])
    ag = AG[...]
    for c in range(2):
        at = pl.ds(1024 * c, 1024)
        from_neigh = dot(ag, B[at, :], 1, 1) * inv_fan
        if c == 0:
            wait_recv(HO_X, HOS.at[0:15])
        PP[0, y, :, at] = jnp.where(FP[:, at] > 0, HO[:, at].astype(F32) + from_neigh, 0.0).astype(BF)
        piece = PP.at[0, y, :, at]
        for yp in YS:
            rcopy(PRE_X, piece, piece, by_y(yp)).start()
    owe(PRE_X, PP.at[0, 0:3])
    wait_recv(FX_X, FX.at[0:2])
    from_behind, from_ahead = FX.at[behind, :, 0:1024], FX.at[ahead, :, 1024:2048]
    rcopy(FY_X, from_behind, from_behind, by_x(ahead)).start()
    rcopy(FY_X, from_ahead, from_ahead, by_x(behind)).start()
    owe(FY_X, FX.at[0])
    wait_recv(R1_X, GWS.at[0:15])
    wait_recv(L1_X, LSR.at[0:15])
    rows = GWR[0].astype(F32)
    part = LSR[0]
    for p in range(1, 16):
        rows = rows + GWR[p].astype(F32)
        part = part + LSR[p]
    for t in range(8):
        T8[t] = rows[8 * t:8 * t + 8]
    L2S[...] = part
    send(R2_X, DP, lambda d: T8.at[lax.div(d, 2)], TR.at[md], by_dp, TR.at[0:15])
    send(L2_X, DP, lambda d: L2S, L2R.at[md], by_dp, L2R.at[0:15])
    TR[md] = T8[z]
    L2R[md] = part

    wait_recv(PRE_X, PP.at[0, 0:3])
    pre = PP[0].reshape(64, 2048)
    for c in range(4):
        at = pl.ds(512 * c, 512)
        PP[1, :, :, at] = (dot(pre, B[at, :], 1, 1) * inv_fan).astype(BF).reshape(4, 16, 512)
    wait_recv(R2_X, TR.at[0:15])
    AW[me, z] = jnp.sum(TR[...], axis=0).astype(BF)
    send(R3_X, ZS, lambda zp: AW.at[me, z], AW.at[me, z], by_z, AW.at[0, 0:7])

    wait_recv(FY_X, FX.at[0])
    full = dot(FX[...].reshape(256, 2048), PP[...].reshape(128, 2048), 1, 1)
    for d in range(16):
        for xs in range(4):
            GS[d, 4 * xs:4 * xs + 4, :] = full[64 * xs + 4 * d:64 * xs + 4 * d + 4, :].astype(BF)
    send(D_X, DP, lambda d: GS.at[d], GR.at[md], by_dp, GS.at[0:15])
    GR[md] = GS[md]

    wait_recv(R3_X, AW.at[0, 0:7])
    send(R4_X, FEAT, lambda p: AW.at[me], AW.at[me], by_feat, AW.at[0:15])
    wait_recv(L2_X, L2R.at[0:15])
    totals = jnp.sum(jnp.sum(L2R[...], axis=0), axis=1, keepdims=True)
    loss_total, norm_total = totals[0:1, :], totals[1:2, :]
    scale = 1.0 / norm_total
    loss_ref[...] = loss_total / norm_total

    wait_recv(D_X, GS.at[0:15])
    summed = GR[0].astype(F32)
    for d in range(1, 16):
        summed = summed + GR[d].astype(F32)
    summed = summed * scale
    for xs in range(4):
        RSS[xs, 0:4, :] = summed[4 * xs:4 * xs + 4, :]
    send(X_X, XS, lambda xp: RSS.at[xp], RX.at[x], by_x, RSS.at[0:3])
    RX[x] = RSS[x]
    wait_recv(R4_X, AW.at[0:15])
    classes = gw2_ref.shape[0]
    for p in range(16):
        for t in range(8):
            row = 64 * (p // 4) + 8 * t
            n = min(8, classes - row)
            if n > 0:
                gw2_ref[row:row + n, (p % 4) // 2, 128 * (p % 2):128 * (p % 2) + 128] = (
                    AW[p, t].astype(F32) * scale)[0:n]
    wait_recv(X_X, RSS.at[0:3])
    left = lax.broadcasted_iota(jnp.int32, (8, 128), 1) < 64
    for pair in range(2):
        a, b = RX[2 * pair], RX[2 * pair + 1]
        at = slice(128 * pair, 128 * pair + 128)
        gw1_ref[0, :, at] = jnp.where(left, a, pltpu.roll(b, 64, 1))[0:4]
        gw1_ref[1, :, at] = jnp.where(left, pltpu.roll(a, 64, 1), b)[0:4]
    for wait in drains:
        wait()


def on_device(features, neighbors, labels, loss_weight, w1_self, w1_neigh, w2_self, w2_neigh):
    fan = neighbors.shape[1]
    vmem = pl.BlockSpec(memory_space=pltpu.VMEM)
    hbm = pl.BlockSpec(memory_space=pltpu.HBM)
    S = pltpu.VMEM
    loss, grad_w1, grad_w2 = pl.pallas_call(
        functools.partial(kernel, fan),
        out_shape=(
            jax.ShapeDtypeStruct((1, 1), F32),
            jax.ShapeDtypeStruct((2, 4, 256), F32),
            jax.ShapeDtypeStruct((w2_self.shape[1], 2, 256), F32),
        ),
        in_specs=[hbm] * 8,
        out_specs=(vmem, vmem, vmem),
        scratch_shapes=[
            S((2048, 2048), BF),
            S((4, 64, 2048), BF),
            S((16, 64, 128), BF),
            S((2, 4, 4, 64, 256), BF),
            S((16, 16, 128), F32),
            S((16, 16, 128), BF),
            S((16, 2048), F32),
            S((16, 2048), BF),
            S((16, 2048), F32),
            S((16, 2048), BF),
            S((16, 2048), BF),
            S((16, 16, 128), BF),
            S((16, 16, 128), BF),
            S((256, 128), BF),
            S((16, 16, 128), BF),
            S((16, 16, 128), BF),
            S((16, 2048), BF),
            S((16, 2048), BF),
            S((2, 4, 16, 2048), BF),
            S((16, 16, 128), BF),
            S((16, 16, 128), BF),
            S((4, 8, 128), F32),
            S((4, 8, 128), F32),
            S((16, 64, 128), BF),
            S((16, 64, 128), BF),
            S((8, 128), F32),
            S((16, 8, 128), F32),
            S((8, 8, 128), F32),
            S((16, 8, 128), F32),
            S((8, 128), F32),
            S((16, 8, 128), F32),
            S((16, 8, 8, 128), BF),
            S((fan, 2048), jnp.int32),
            S((16, 128), jnp.int32),
            S((16, 128), F32),
            S(w2_self.shape[::-1], BF),
            S(w2_neigh.shape[::-1], BF),
            pltpu.SemaphoreType.DMA((2, 23)),
            pltpu.SemaphoreType.DMA((7,)),
        ],
        compiler_params=pltpu.CompilerParams(
            collective_id=0, has_side_effects=True, vmem_limit_bytes=40 * 2 ** 20),
        name="sage_step",
    )(*(pltpu.with_memory_space_constraint(a, pltpu.HBM) for a in (
        features, neighbors.T, labels.reshape(16, 128), loss_weight.reshape(16, 128),
        w1_self, w1_neigh, w2_self.T, w2_neigh.T)))
    return loss.reshape(()), grad_w1, grad_w2.transpose(1, 2, 0)


def solution(mesh):
    in_specs = (
        P("feat", "dp"),
        P("dp", None),
        P("dp"),
        P("dp"),
        P("feat", None),
        P("feat", None),
        P(),
        P(),
    )
    out_specs = (P(), P(None, ("feat", "dp"), None), P())
    return jax.shard_map(
        on_device, mesh=mesh, in_specs=in_specs, out_specs=out_specs, check_vma=False
    )
```

```python
import functools

import jax
import jax.numpy as jnp
from jax import lax
from jax.experimental import pallas as pl
from jax.experimental.pallas import tpu as pltpu
from jax.sharding import PartitionSpec as P

BF = jnp.bfloat16
F32 = jnp.float32

(WA_X, WB_X, WC_X, WD_X, FWD_X, F_X, PS_X, PN_X, H_X, S_X, HO_X, AG_X, PRE_X, FX_X, FY_X,
 D_X, X_X, R1_X, L1_X, R2_X, L2_X, R3_X, R4_X) = range(23)


def dot(a, b, ca, cb):
    return lax.dot_general(a, b, (((ca,), (cb,)), ((), ())), preferred_element_type=F32)


def lanes(p, width=128):
    return pl.ds(pl.multiple_of(p * width, width), width)


def kernel(fan, f_hbm, nbr_hbm, lab_hbm, lw_hbm, ws_hbm, wn_hbm, w2s_hbm, w2n_hbm,
           loss_ref, gw1_ref, gw2_ref,
           B, FX, FO, WG, PSS, PNS, PS, PN, FP, HC, SC, HT, SA, GT, HOS, AGS, HO, AG,
           PP, GS, GR, RSS, RX, GWS, GWR, LSS, LSR, T8, TR, L2S, L2R, AW,
           nbr_ref, lab_ref, lw_ref, w2s_ref, w2n_ref, sems, lsem):
    me, md = lax.axis_index("feat"), lax.axis_index("dp")
    x, y = lax.rem(me, 4), lax.div(me, 4)
    core, z = lax.rem(md, 2), lax.div(md, 2)
    mate = (me, md + 1 - 2 * core)
    inv_fan = 1.0 / fan

    def order(p):
        return lax.rem(p, 4) * 4 + lax.div(p, 4)

    q_me = order(me)

    near = lambda d, n: min(d, n - d)
    XS = [lax.rem(x + d, 4) for d in (2, 1, 3)]
    YS = [lax.rem(y + d, 4) for d in (2, 1, 3)]
    ZS = [lax.rem(z + d, 8) for d in (4, 3, 5, 2, 6, 1, 7)]
    plane = sorted(((a, b) for a in range(4) for b in range(4) if a or b),
                   key=lambda o: -near(o[0], 4) - near(o[1], 4))
    FEAT = [lax.rem(y + a, 4) * 4 + lax.rem(x + b, 4) for a, b in plane]
    line = sorted(((a, b) for a in range(8) for b in range(2) if a or b),
                  key=lambda o: -near(o[0], 8))
    DP = [lax.rem(z + a, 8) * 2 + (core if b == 0 else 1 - core) for a, b in line]

    def rcopy(row, src, dst, dev):
        return pltpu.make_async_remote_copy(
            src_ref=src, dst_ref=dst, send_sem=sems.at[0, row], recv_sem=sems.at[1, row],
            device_id=dev, device_id_type=pl.DeviceIdType.MESH)

    by_feat = lambda p: (p, md)
    by_dp = lambda d: (me, d)
    by_x = lambda xp: (y * 4 + xp, md)
    by_y = lambda yp: (yp * 4 + x, md)
    by_z = lambda zp: (me, zp * 2 + core)
    drains = []

    def owe(row, view):
        drains.append(lambda: rcopy(row, view, view, mate).wait_send())

    def send(row, peers, src, dst, dev, view):
        for p in peers:
            rcopy(row, src(p), dst, dev(p)).start()
        owe(row, view)

    def wait_recv(row, view):
        rcopy(row, view, view, mate).wait_recv()

    bar = pltpu.get_barrier_semaphore()
    mesh_id = pl.DeviceIdType.MESH
    for p in FEAT:
        pl.semaphore_signal(bar, 1, device_id=by_feat(p), device_id_type=mesh_id)
    for d in DP:
        pl.semaphore_signal(bar, 1, device_id=by_dp(d), device_id_type=mesh_id)

    local = [
        pltpu.make_async_copy(f_hbm, FX.at[x], lsem.at[1]),
        pltpu.make_async_copy(nbr_hbm, nbr_ref, lsem.at[2]),
        pltpu.make_async_copy(lab_hbm, lab_ref, lsem.at[3]),
        pltpu.make_async_copy(lw_hbm, lw_ref, lsem.at[4]),
        pltpu.make_async_copy(w2s_hbm, w2s_ref, lsem.at[5]),
        pltpu.make_async_copy(w2n_hbm, w2n_ref, lsem.at[6]),
    ]
    own_w = pltpu.make_async_copy(ws_hbm, WG.at[core, y, x], lsem.at[0])

    @pl.when(core == 0)
    def _():
        own_w.start()

    @pl.when(core == 1)
    def _():
        pltpu.make_async_copy(wn_hbm, WG.at[core, y, x], lsem.at[0]).start()

    for c in local:
        c.start()
    own_w.wait()
    local[0].wait()
    pl.semaphore_wait(bar, 30)

    upper, lower = WG.at[core, y, x, 0:32], WG.at[core, y, x, 32:64]
    send(WA_X, XS, lambda xp: upper, upper, by_x, WG.at[0, 0, 0:3, 0:32])
    send(WB_X, YS, lambda yp: lower, lower, by_y, WG.at[0, 0, 0:3, 32:64])
    send(F_X, FEAT, lambda p: FX.at[x, :, lanes(p)], FO.at[me], by_feat, FO.at[0:15])
    for c in local[1:]:
        c.wait()
    FO[me] = FX[x, :, lanes(me)]
    GT[...] = jnp.zeros_like(GT)
    RSS[...] = jnp.zeros_like(RSS)
    LSS[...] = jnp.zeros_like(LSS)

    iota = lax.broadcasted_iota(jnp.int32, (256, 128), 0).astype(F32).astype(BF).reshape(16, 16, 128)

    def spread(row):
        return jnp.broadcast_to(row.astype(F32), (16, 128)).astype(BF)

    def build(t, carry):
        lo = lanes(t)
        ids = nbr_ref[:, lo]
        times = jnp.zeros((fan, 128), F32)
        for k in range(fan):
            times = times + jnp.where(ids == ids[k:k + 1], 1.0, 0.0)
        count = [spread(times[k:k + 1]) for k in range(fan)]
        low = [spread(ids[k:k + 1] & 255) for k in range(fan)]
        high = [spread(ids[k:k + 1] >> 8) for k in range(fan)]

        def group(g, inner):
            here = jnp.full((16, 128), g, jnp.int32).astype(F32).astype(BF)
            acc = jnp.zeros((16, 16, 128), BF)
            for k in range(fan):
                at = jnp.where(high[k] == here, low[k], BF(300))
                acc = jnp.where(iota == at[None], count[k][None], acc)
            B[lanes(g, 256), lo] = acc.reshape(256, 128)
            return inner

        return lax.fori_loop(0, 8, group, carry)

    lax.fori_loop(0, 6, build, 0)
    wait_recv(WA_X, WG.at[0, 0, 0:3, 0:32])
    wait_recv(WB_X, WG.at[0, 0, 0:3, 32:64])
    uppers, lowers = WG.at[core, y, :, 0:32], WG.at[core, :, x, 32:64]
    send(WC_X, YS, lambda yp: uppers, uppers, by_y, WG.at[0, 0:3, :, 0:32])
    send(WD_X, XS, lambda xp: lowers, lowers, by_x, WG.at[0, :, 0:3, 32:64])
    for ready in (uppers, lowers):
        rcopy(FWD_X, ready, ready, mate).start()
    lax.fori_loop(6, 14, build, 0)
    wait_recv(WC_X, WG.at[0, 0:3, :, 0:32])
    for yp in YS:
        ready = WG.at[core, yp, :, 0:32]
        rcopy(FWD_X, ready, ready, mate).start()
    wait_recv(WD_X, WG.at[0, :, 0:3, 32:64])
    for xp in XS:
        ready = WG.at[core, :, xp, 32:64]
        rcopy(FWD_X, ready, ready, mate).start()
    owe(FWD_X, WG.at[0])
    lax.fori_loop(14, 16, build, 0)
    wait_recv(F_X, FO.at[0:15])
    wait_recv(FWD_X, WG.at[0])

    fo = FO[...].reshape(1024, 128)
    PNS[...] = dot(WG[1].reshape(1024, 256), fo, 0, 0).astype(BF).reshape(16, 16, 128)
    send(PN_X, FEAT, lambda p: PNS.at[order(p)], PN.at[:, lanes(me)], by_feat, PNS.at[0:15])
    PSS[...] = dot(WG[0].reshape(1024, 256), fo, 0, 0).reshape(16, 16, 128)
    send(PS_X, FEAT, lambda p: PSS.at[order(p)], PS.at[:, lanes(me)], by_feat, PSS.at[0:15])
    PN[:, lanes(me)] = PNS[q_me]
    PS[:, lanes(me)] = PSS[q_me]

    def features_to(xp, piece):
        part = FX.at[x, :, lanes(piece, 512)]
        rcopy(FX_X, part, part, by_x(xp)).start()

    ahead, behind = lax.rem(x + 1, 4), lax.rem(x + 3, 4)
    features_to(ahead, 0)
    features_to(behind, 0)
    wait_recv(PN_X, PNS.at[0:15])
    features_to(ahead, 1)
    features_to(behind, 1)
    mean = dot(PN[...], B[...], 1, 0) * inv_fan
    wait_recv(PS_X, PSS.at[0:15])
    first = PS[...] + mean
    FP[...] = first
    hc = jnp.maximum(first, 0.0).astype(BF)
    HC[...] = hc
    send(H_X, FEAT, lambda p: HC.at[:, lanes(p)], HT.at[q_me], by_feat, HT.at[0:15])
    HT[q_me] = HC[:, lanes(me)]

    for s in range(4):
        c = lax.rem(y + 1 + s, 4)
        SC[:, lanes(c, 512)] = (dot(hc, B[:, lanes(c, 512)], 1, 0) * inv_fan).astype(BF)
        for p in (4 * c, 4 * c + 1, 4 * c + 2, 4 * c + 3):
            @pl.when(p != me)
            def _(p=p):
                rcopy(S_X, SC.at[:, lanes(p)], SA.at[q_me], by_feat(p)).start()

    owe(S_X, SA.at[0:15])
    for piece in (2, 3):
        features_to(ahead, piece)
        features_to(behind, piece)
    owe(FX_X, FX.at[0:2])
    SA[q_me] = SC[:, lanes(me)]
    wait_recv(H_X, HT.at[0:15])
    ht = HT[...].reshape(256, 128)
    w2s, w2n = w2s_ref[...], w2n_ref[...]
    from_self = dot(w2s, ht, 1, 0)
    wait_recv(S_X, SA.at[0:15])

    sa = SA[...].reshape(256, 128)
    logits = from_self + dot(w2n, sa, 1, 0)
    top = jnp.max(logits, axis=0, keepdims=True)
    shifted = logits - top
    logprob = shifted - jnp.log(jnp.sum(jnp.exp(shifted), axis=0, keepdims=True))
    hot = lax.broadcasted_iota(jnp.int32, logits.shape, 0) == lab_ref[pl.ds(me, 1), :]
    picked = jnp.sum(jnp.where(hot, logprob, 0.0), axis=0, keepdims=True)
    weight = lw_ref[pl.ds(me, 1), :]
    chance = jnp.exp(picked)
    rest = 1.0 - chance
    slope = weight * (2.0 * rest * chance * picked - rest * rest)
    grad = (slope * (jnp.where(hot, 1.0, 0.0) - jnp.exp(logprob))).astype(BF)
    AGS[...] = dot(w2n, grad, 0, 0).astype(BF).reshape(16, 16, 128)
    send(AG_X, FEAT, lambda p: AGS.at[order(p)], AG.at[:, lanes(me)], by_feat, AGS.at[0:15])
    HOS[...] = dot(w2s, grad, 0, 0).astype(BF).reshape(16, 16, 128)
    send(HO_X, FEAT, lambda p: HOS.at[order(p)], HO.at[:, lanes(me)], by_feat, HOS.at[0:15])
    AG[:, lanes(me)] = AGS[q_me]
    HO[:, lanes(me)] = HOS[q_me]
    GT[0:grad.shape[0], :] = grad
    gt = GT[...]
    for part, table in enumerate((ht, sa)):
        second = dot(gt, table, 1, 1).astype(BF)
        for r in range(4):
            for c in range(2):
                GWS[4 * r + 2 * part + c] = second[64 * r:64 * r + 64, 128 * c:128 * c + 128]
    send(R1_X, FEAT, lambda p: GWS.at[p], GWR.at[me], by_feat, GWS.at[0:15])
    GWR[me] = GWS[me]
    LSS[0:1, :] = -rest * rest * picked * weight
    LSS[1:2, :] = weight
    send(L1_X, FEAT, lambda p: LSS, LSR.at[me], by_feat, LSR.at[0:15])
    LSR[me] = LSS[...]
    wait_recv(AG_X, AGS.at[0:15])
    ag = AG[...]
    for c in range(2):
        at = pl.ds(1024 * c, 1024)
        from_neigh = dot(ag, B[at, :], 1, 1) * inv_fan
        if c == 0:
            wait_recv(HO_X, HOS.at[0:15])
        PP[0, y, :, at] = jnp.where(FP[:, at] > 0, HO[:, at].astype(F32) + from_neigh, 0.0).astype(BF)
        piece = PP.at[0, y, :, at]
        for yp in YS:
            rcopy(PRE_X, piece, piece, by_y(yp)).start()
    owe(PRE_X, PP.at[0, 0:3])
    wait_recv(FX_X, FX.at[0:2])
    from_behind, from_ahead = FX.at[behind, :, 0:1024], FX.at[ahead, :, 1024:2048]
    rcopy(FY_X, from_behind, from_behind, by_x(ahead)).start()
    rcopy(FY_X, from_ahead, from_ahead, by_x(behind)).start()
    owe(FY_X, FX.at[0])
    wait_recv(R1_X, GWS.at[0:15])
    wait_recv(L1_X, LSR.at[0:15])
    rows = GWR[0].astype(F32)
    part = LSR[0]
    for p in range(1, 16):
        rows = rows + GWR[p].astype(F32)
        part = part + LSR[p]
    for t in range(8):
        T8[t] = rows[8 * t:8 * t + 8]
    L2S[...] = part
    send(R2_X, DP, lambda d: T8.at[lax.div(d, 2)], TR.at[md], by_dp, TR.at[0:15])
    send(L2_X, DP, lambda d: L2S, L2R.at[md], by_dp, L2R.at[0:15])
    TR[md] = T8[z]
    L2R[md] = part

    wait_recv(PRE_X, PP.at[0, 0:3])
    pre = PP[0].reshape(64, 2048)
    for c in range(2):
        at = pl.ds(1024 * c, 1024)
        PP[1, :, :, at] = (dot(pre, B[at, :], 1, 1) * inv_fan).astype(BF).reshape(4, 16, 1024)
    wait_recv(R2_X, TR.at[0:15])
    AW[me, z] = jnp.sum(TR[...], axis=0).astype(BF)
    send(R3_X, ZS, lambda zp: AW.at[me, z], AW.at[me, z], by_z, AW.at[0, 0:7])

    wait_recv(FY_X, FX.at[0])
    full = dot(FX[...].reshape(256, 2048), PP[...].reshape(128, 2048), 1, 1)
    for d in range(16):
        for xs in range(4):
            GS[d, 4 * xs:4 * xs + 4, :] = full[64 * xs + 4 * d:64 * xs + 4 * d + 4, :].astype(BF)
    send(D_X, DP, lambda d: GS.at[d], GR.at[md], by_dp, GS.at[0:15])
    GR[md] = GS[md]

    wait_recv(R3_X, AW.at[0, 0:7])
    send(R4_X, FEAT, lambda p: AW.at[me], AW.at[me], by_feat, AW.at[0:15])
    wait_recv(L2_X, L2R.at[0:15])
    totals = jnp.sum(jnp.sum(L2R[...], axis=0), axis=1, keepdims=True)
    loss_total, norm_total = totals[0:1, :], totals[1:2, :]
    scale = 1.0 / norm_total
    loss_ref[...] = loss_total / norm_total

    wait_recv(D_X, GS.at[0:15])
    summed = GR[0].astype(F32)
    for d in range(1, 16):
        summed = summed + GR[d].astype(F32)
    summed = summed * scale
    for xs in range(4):
        RSS[xs, 0:4, :] = summed[4 * xs:4 * xs + 4, :]
    send(X_X, XS, lambda xp: RSS.at[xp], RX.at[x], by_x, RSS.at[0:3])
    RX[x] = RSS[x]
    wait_recv(R4_X, AW.at[0:15])
    classes = gw2_ref.shape[0]
    for p in range(16):
        for t in range(8):
            row = 64 * (p // 4) + 8 * t
            n = min(8, classes - row)
            if n > 0:
                gw2_ref[row:row + n, (p % 4) // 2, 128 * (p % 2):128 * (p % 2) + 128] = (
                    AW[p, t].astype(F32) * scale)[0:n]
    wait_recv(X_X, RSS.at[0:3])
    left = lax.broadcasted_iota(jnp.int32, (8, 128), 1) < 64
    for pair in range(2):
        a, b = RX[2 * pair], RX[2 * pair + 1]
        at = slice(128 * pair, 128 * pair + 128)
        gw1_ref[0, :, at] = jnp.where(left, a, pltpu.roll(b, 64, 1))[0:4]
        gw1_ref[1, :, at] = jnp.where(left, pltpu.roll(a, 64, 1), b)[0:4]
    for wait in drains:
        wait()


def on_device(features, neighbors, labels, loss_weight, w1_self, w1_neigh, w2_self, w2_neigh):
    fan = neighbors.shape[1]
    vmem = pl.BlockSpec(memory_space=pltpu.VMEM)
    hbm = pl.BlockSpec(memory_space=pltpu.HBM)
    S = pltpu.VMEM
    loss, grad_w1, grad_w2 = pl.pallas_call(
        functools.partial(kernel, fan),
        out_shape=(
            jax.ShapeDtypeStruct((1, 1), F32),
            jax.ShapeDtypeStruct((2, 4, 256), F32),
            jax.ShapeDtypeStruct((w2_self.shape[1], 2, 256), F32),
        ),
        in_specs=[hbm] * 8,
        out_specs=(vmem, vmem, vmem),
        scratch_shapes=[
            S((2048, 2048), BF),
            S((4, 64, 2048), BF),
            S((16, 64, 128), BF),
            S((2, 4, 4, 64, 256), BF),
            S((16, 16, 128), F32),
            S((16, 16, 128), BF),
            S((16, 2048), F32),
            S((16, 2048), BF),
            S((16, 2048), F32),
            S((16, 2048), BF),
            S((16, 2048), BF),
            S((16, 16, 128), BF),
            S((16, 16, 128), BF),
            S((256, 128), BF),
            S((16, 16, 128), BF),
            S((16, 16, 128), BF),
            S((16, 2048), BF),
            S((16, 2048), BF),
            S((2, 4, 16, 2048), BF),
            S((16, 16, 128), BF),
            S((16, 16, 128), BF),
            S((4, 8, 128), F32),
            S((4, 8, 128), F32),
            S((16, 64, 128), BF),
            S((16, 64, 128), BF),
            S((8, 128), F32),
            S((16, 8, 128), F32),
            S((8, 8, 128), F32),
            S((16, 8, 128), F32),
            S((8, 128), F32),
            S((16, 8, 128), F32),
            S((16, 8, 8, 128), BF),
            S((fan, 2048), jnp.int32),
            S((16, 128), jnp.int32),
            S((16, 128), F32),
            S(w2_self.shape[::-1], BF),
            S(w2_neigh.shape[::-1], BF),
            pltpu.SemaphoreType.DMA((2, 23)),
            pltpu.SemaphoreType.DMA((7,)),
        ],
        compiler_params=pltpu.CompilerParams(
            collective_id=0, has_side_effects=True, vmem_limit_bytes=40 * 2 ** 20),
        name="sage_step",
    )(*(pltpu.with_memory_space_constraint(a, pltpu.HBM) for a in (
        features, neighbors.T, labels.reshape(16, 128), loss_weight.reshape(16, 128),
        w1_self, w1_neigh, w2_self.T, w2_neigh.T)))
    return loss.reshape(()), grad_w1, grad_w2.transpose(1, 2, 0)


def solution(mesh):
    in_specs = (
        P("feat", "dp"),
        P("dp", None),
        P("dp"),
        P("dp"),
        P("feat", None),
        P("feat", None),
        P(),
        P(),
    )
    out_specs = (P(), P(None, ("feat", "dp"), None), P())
    return jax.shard_map(
        on_device, mesh=mesh, in_specs=in_specs, out_specs=out_specs, check_vma=False
    )
```
